128 devices in a mesh: section: 4 (over z_lo, core), seq: 16 (over x, y), head: 2 (over z_hi).
Axes of the slice: x: 4, y: 4, z: 4 (z_hi: 2, z_lo: 2; z = z_hi * 2 + z_lo), core: 2. Of those that a mesh axis runs over, the one named last changes fastest.
Arguments:
- text_hidden: bfloat16 [16384, 4096], P('seq'), may hold values from -600 to 600
- norm_gain: float32 [4096], replicated, may hold values from 0.1 to 1.9
- image_features: bfloat16 [32768, 1024], P('seq'), may hold values from -6 to 6
- query_weight: bfloat16 [4096, 4096], P(None, ('section', 'head')), may hold values from -30 to 30
- key_weight: bfloat16 [1024, 1024], P(None, ('section', 'head')), may hold values from -0.75 to 0.75
- value_weight: bfloat16 [1024, 1024], P(None, ('section', 'head')), may hold values from -0.1875 to 0.1875
- output_weight: bfloat16 [4096, 4096], P(('section', 'head')), may hold values from -0.125 to 0.125
- selected: int32 [128, 16], P('seq'), may hold values from 0 to 511, as said below
Outputs:
- attn_output: bfloat16 [16384, 4096], P('seq', ('section', 'head'))
The draws below stay inside these ranges and needn't reach their ends.
Inputs may be any that keep to these rules, and one draw needn't show every extreme that they name: `selected`: each row names 16 different image blocks. The tiles of one seq index together select at most 8 different blocks from the 32 blocks of any one seq index, and exactly 8 from some seq index.
All inputs are finite; a program needn't handle non-finite values.
Results may differ from the reference program's by a relative error of at most 0.0069.
The reference program's roundings to bfloat16 on the way (of `normed`, `queries`, `weights` and `attended`) count: a program that leaves them out, or rounds other values in their place, can miss the bound.
Values may be sent and summed in bfloat16 or wider, within the bound.
No kernel may reach another device: no remote copies, remote signals or barrier semaphores. Data moves between devices by JAX's collectives and lax.ppermute only.
A program may use at most 128 MiB of HBM per device.

```python
import jax
import jax.numpy as jnp
from jax import lax

D = 4096
HEADS = 32
KV_HEADS = 8
HEAD_DIM = 128
ENC = 1024
TILE = 128
BLOCK = 64
TOPK = 16
BLOCKS_DEV = 32
TEXT = 16384
TILES = 128
BLOCKS = 512
IMAGE = 32768
CAP = 8
N_SEQ = 16


def draw_text_hidden(key, part):
    first_key = jax.random.fold_in(jax.random.fold_in(key, 11), 0)
    sample = jnp.clip(jax.random.normal(first_key, (TEXT, D), jnp.float32), -6.0, 6.0)
    return sample.astype(jnp.bfloat16)


def draw_query_weight(key, part):
    first_key = jax.random.fold_in(jax.random.fold_in(key, 23), 0)
    sample = jnp.clip(jax.random.normal(first_key, (D, HEADS * HEAD_DIM), jnp.float32), -6.0, 6.0) * D ** (-0.5)
    return sample.astype(jnp.bfloat16)


def pick_for_device(device_key):
    owner_key, local_key, start_key = jax.random.split(device_key, 3)
    owners = jax.random.permutation(owner_key, N_SEQ).astype(jnp.int32)
    local_keys = jax.random.split(local_key, N_SEQ)
    locals_all = jax.vmap(lambda one_key: jax.random.permutation(one_key, BLOCKS_DEV)[:CAP].astype(jnp.int32))(local_keys)
    union = (owners[:, None] * BLOCKS_DEV + locals_all).reshape(N_SEQ * CAP)
    tiles_dev = TILES // N_SEQ
    rotation = jax.random.randint(start_key, (), 0, N_SEQ).astype(jnp.int32) * CAP
    position = (rotation + jnp.arange(tiles_dev, dtype=jnp.int32)[:, None] * TOPK + jnp.arange(TOPK, dtype=jnp.int32)[None, :]) % (N_SEQ * CAP)
    return union[position]


def draw_selected(key, part):
    device_keys = jax.random.split(jax.random.fold_in(key, 37), N_SEQ)
    picked = jax.vmap(pick_for_device)(device_keys)
    return picked.reshape(TILES, TOPK).astype(jnp.int32)


def with_spikes(entries, stream_key, source, target, parts, factor):
    def block_of(axis_at):
        return (jnp.arange(entries.shape[axis_at]) // (entries.shape[axis_at] // parts)).reshape((-1,) + (1,) * (entries.ndim - 1 - axis_at))

    first = jax.random.permutation(stream_key, parts)[block_of(target)]
    other_side = (block_of(target) + parts // 2) % parts
    return jnp.where((block_of(source) == first) | (block_of(source) == other_side), factor * entries, entries)


def levels(rng, shape, cuts, low, high):
    def one(dim, parts):
        heights = jax.random.uniform(jax.random.fold_in(jax.random.fold_in(rng, 6), dim), (parts,), jnp.float32, low / len(cuts), high / len(cuts))
        return jnp.repeat(jnp.exp(heights), shape[dim] // parts).reshape((-1,) + (1,) * (len(shape) - dim - 1))

    level = one(*cuts[0])
    for cut in cuts[1:]:
        level = level * one(*cut)
    return level


def scatter_about(own_key, shape, scale, limit, cuts=(), kind=jnp.bfloat16):
    entries = jax.random.normal(own_key, shape, jnp.float32) * scale
    if len(cuts) > 0:
        entries = levels(own_key, shape, cuts, -0.22, 0.18) * entries
    return jnp.clip(entries, min=-limit, max=limit).astype(kind)


def bell_draw_with(rng, extent, width, reach, pieces, heavy, held_as=jnp.bfloat16):
    result = width * jax.random.normal(rng, extent, jnp.float32)
    if pieces:
        result = result * levels(rng, extent, pieces, -0.22, 0.18)
    return jnp.clip(with_spikes(result, jax.random.fold_in(rng, 3), *heavy), -reach, reach).astype(held_as)


def setup_inputs(seed: int = 0) -> dict:
    arg_keys = jax.random.split(jax.random.key(seed), 9)
    return {
        "text_hidden": draw_text_hidden(jax.random.fold_in(arg_keys[8], 71), 0),
        "norm_gain": jnp.clip(1.0 + 0.18 * jax.random.normal(arg_keys[1], (D,), jnp.float32), 0.1, 1.9),
        "image_features": scatter_about(arg_keys[2], (IMAGE, ENC), 1.0, 6.0, ((0, 16),)),
        "query_weight": draw_query_weight(jax.random.fold_in(arg_keys[8], 71), 0),
        "key_weight": scatter_about(arg_keys[4], (ENC, KV_HEADS * HEAD_DIM), (ENC // 16) ** -0.5, 0.75, ((1, 8),)),
        "value_weight": scatter_about(arg_keys[5], (ENC, KV_HEADS * HEAD_DIM), ENC ** -0.5, 0.1875, ((1, 8),)),
        "output_weight": bell_draw_with(arg_keys[6], (HEADS * HEAD_DIM, D), (HEADS * HEAD_DIM) ** -0.5, 0.125, ((0, 8),), (0, 1, 8, 2.0)),
        "selected": draw_selected(jax.random.fold_in(arg_keys[8], 71), 0),
    }


EPSILON = 1e-05

def reference(text_hidden, norm_gain, image_features, query_weight, key_weight, value_weight, output_weight, selected):
    as_float = text_hidden.astype(jnp.float32)
    inverse = lax.rsqrt(lax.optimization_barrier(jnp.mean(as_float * as_float, axis=-1, keepdims=True)) + EPSILON)
    normed = (as_float * inverse * norm_gain).astype(jnp.bfloat16)
    queries = jnp.dot(normed, query_weight, preferred_element_type=jnp.float32).astype(jnp.bfloat16)
    key_rows = jnp.dot(image_features, key_weight, preferred_element_type=jnp.float32).astype(jnp.bfloat16)
    value_rows = jnp.dot(image_features, value_weight, preferred_element_type=jnp.float32).astype(jnp.bfloat16)
    group_size = HEADS // KV_HEADS
    key_blocks = key_rows.reshape(BLOCKS, BLOCK, KV_HEADS, HEAD_DIM)
    value_blocks = value_rows.reshape(BLOCKS, BLOCK, KV_HEADS, HEAD_DIM)
    query_tiles = queries.reshape(TILES, TILE, KV_HEADS, group_size, HEAD_DIM)

    def one_tile(tile_input):
        tile_queries, picked = tile_input
        tile_keys = key_blocks[picked].reshape(TOPK * BLOCK, KV_HEADS, HEAD_DIM).astype(jnp.float32)
        tile_values = value_blocks[picked].reshape(TOPK * BLOCK, KV_HEADS, HEAD_DIM).astype(jnp.float32)
        scores = jnp.einsum('tkgd,skd->kgts', tile_queries.astype(jnp.float32), tile_keys) * HEAD_DIM ** (-0.5)
        largest = lax.optimization_barrier(jnp.max(scores, axis=-1, keepdims=True))
        exponent = jnp.exp(scores - largest)
        weights = (exponent / lax.optimization_barrier(jnp.sum(exponent, axis=-1, keepdims=True))).astype(jnp.bfloat16)
        attended = jnp.einsum('kgts,skd->tkgd', weights.astype(jnp.float32), tile_values)
        return attended.astype(jnp.bfloat16)
    attended = lax.map(one_tile, (query_tiles, selected))
    attended = attended.reshape(TILES * TILE, HEADS * HEAD_DIM)
    return jnp.dot(attended, output_weight, preferred_element_type=jnp.float32).astype(jnp.bfloat16)
```

```python
import functools

import jax
import jax.numpy as jnp
from jax import lax
from jax.experimental import pallas as pl
from jax.experimental.pallas import tpu as pltpu
from jax.sharding import PartitionSpec as P

HEADS = 32
KV_HEADS = 8
HEAD_DIM = 128
GROUP = HEADS // KV_HEADS
TILE = 128
BLOCK = 64
TOPK = 16
SIDE = 4
CAP = 8
PICKS = SIDE * SIDE * CAP
NOTE_ROWS = 16
EPSILON = 1e-05
SCALE = HEAD_DIM**-0.5

SECTION_HEAD = ("section", "head")
VMEM_WHOLE = pl.BlockSpec(memory_space=pltpu.VMEM)
SMEM_WHOLE = pl.BlockSpec(memory_space=pltpu.SMEM)


def along_seq(value, dx, dy):
    pairs = [
        (x * SIDE + y, (x + dx) % SIDE * SIDE + (y + dy) % SIDE)
        for x in range(SIDE)
        for y in range(SIDE)
    ]
    return lax.ppermute(value, "seq", pairs)


def column(z, core):
    return (z % 2) * 4 + core * 2 + z // 2


def along_z(value, place):
    pairs = []
    for z in range(4):
        for core in range(2):
            pairs.append((column(z, core), column(*place(z, core))))
    return lax.ppermute(value, SECTION_HEAD, pairs)


def to_near(value):
    return along_z(value, lambda z, core: (z ^ 1, core))


def to_far(value):
    return along_z(value, lambda z, core: (3 - z, core))


def to_core(value):
    return along_z(value, lambda z, core: (z, 1 - core))


def project_body(ids_ref, x_ref, wk_ref, wv_ref, k_ref, v_ref, slots_ref, w_ref):
    step = pl.program_id(0)
    rows = x_ref.shape[0]
    steps = pl.num_programs(0)
    blocks_dev = (k_ref.shape[0] - NOTE_ROWS) // BLOCK
    blocks = SIDE * SIDE * blocks_dev

    @pl.when(step == 0)
    def _():
        w_ref[:, :HEAD_DIM] = wk_ref[...]
        w_ref[:, HEAD_DIM:] = wv_ref[...]

    @pl.when(step == steps - 1)
    def _():
        ids = ids_ref[...]
        block = lax.broadcasted_iota(jnp.int32, (blocks, PICKS), 0)
        hit = (block == ids).astype(jnp.float32)
        wanted = jnp.broadcast_to(jnp.max(hit, axis=1, keepdims=True), (blocks, PICKS))
        one = lax.broadcasted_iota(jnp.int32, (blocks, blocks), 0)
        other = lax.broadcasted_iota(jnp.int32, (blocks, blocks), 1)
        before = (one // blocks_dev == other // blocks_dev) & (other < one)
        rank = jnp.dot(
            before.astype(jnp.float32).astype(jnp.bfloat16),
            wanted.astype(jnp.bfloat16),
            preferred_element_type=jnp.float32,
        )
        owner = block // blocks_dev
        slot = (owner * CAP).astype(jnp.float32) + rank
        slots = jnp.sum(hit * slot, axis=0, keepdims=True)
        slots_ref[...] = jnp.broadcast_to(slots, slots_ref.shape).astype(jnp.int32)
        place = lax.broadcasted_iota(jnp.int32, (blocks, PICKS), 1).astype(jnp.float32)
        local = (block % blocks_dev).astype(jnp.float32)
        asked = jnp.sum(
            jnp.where(slot == place, wanted * local, 0.0), axis=0, keepdims=True
        )
        note = jnp.broadcast_to(asked, (NOTE_ROWS, PICKS)).astype(jnp.bfloat16)
        k_ref[rows * steps :, :] = note
        v_ref[rows * steps :, :] = note

    both = jnp.dot(x_ref[...], w_ref[...], preferred_element_type=jnp.float32)
    at = pl.ds(pl.multiple_of(step * rows, rows), rows)
    k_ref[at, :] = both[:, :HEAD_DIM].astype(jnp.bfloat16)
    v_ref[at, :] = both[:, HEAD_DIM:].astype(jnp.bfloat16)


def project(image_features, key_weight, value_weight, ids):
    rows, enc = image_features.shape
    steps = 4
    out = jax.ShapeDtypeStruct((rows + NOTE_ROWS, HEAD_DIM), jnp.bfloat16)
    whole = lambda shape: pl.BlockSpec(shape, lambda i: (0,) * len(shape))
    return pl.pallas_call(
        project_body,
        grid=(steps,),
        in_specs=[
            whole((1, PICKS)),
            pl.BlockSpec((rows // steps, enc), lambda i: (i, 0)),
            whole((enc, HEAD_DIM)),
            whole((enc, HEAD_DIM)),
        ],
        out_specs=[
            whole((rows + NOTE_ROWS, HEAD_DIM)),
            whole((rows + NOTE_ROWS, HEAD_DIM)),
            whole((8, PICKS)),
        ],
        out_shape=[out, out, jax.ShapeDtypeStruct((8, PICKS), jnp.int32)],
        scratch_shapes=[pltpu.VMEM((enc, 2 * HEAD_DIM), jnp.bfloat16)],
        compiler_params=pltpu.CompilerParams(vmem_limit_bytes=40 << 20),
        cost_estimate=pl.CostEstimate(
            flops=4 * rows * enc * HEAD_DIM, bytes_accessed=2 * rows * enc, transcendentals=0
        ),
        name="project",
    )(ids, image_features, key_weight, value_weight)


def pack_body(ask_ref, place_ref, own, plus, two_low, two_high, minus, out0, out1, out2, out3):
    me, base, stride = place_ref[0], place_ref[1], place_ref[2]
    half = two_low.shape[0] // BLOCK
    for dest, out in enumerate((out0, out1, out2, out3)):
        for away in range(SIDE):
            first = base + ((me + away) & (SIDE - 1)) * stride
            for slot in range(CAP):
                block = ask_ref[dest, first + slot]

                def rows(ref, index):
                    return ref[pl.ds(pl.multiple_of(index * BLOCK, BLOCK), BLOCK), :]

                if away == 0:
                    value = rows(own, block)
                elif away == 1:
                    value = rows(plus, block)
                elif away == 3:
                    value = rows(minus, block)
                else:
                    value = jnp.where(
                        block < half,
                        rows(two_low, jnp.minimum(block, half - 1)),
                        rows(two_high, jnp.maximum(block - half, 0)),
                    )
                out[(away * CAP + slot) * BLOCK : (away * CAP + slot + 1) * BLOCK, :] = value


def pack(ask, place, own, plus, two_low, two_high, minus):
    out = jax.ShapeDtypeStruct((SIDE * CAP * BLOCK, HEAD_DIM), jnp.bfloat16)
    return pl.pallas_call(
        pack_body,
        in_specs=[SMEM_WHOLE, SMEM_WHOLE] + [VMEM_WHOLE] * 5,
        out_specs=[VMEM_WHOLE] * SIDE,
        out_shape=[out] * SIDE,
        compiler_params=pltpu.CompilerParams(vmem_limit_bytes=24 << 20),
        name="pack",
    )(ask, place, own, plus, two_low, two_high, minus)


def attend_body(first_tile, slots_ref, place_ref, q_ref, k_ref, v_ref, o_ref, kt, vt):
    my_x, my_y = place_ref[0], place_ref[1]
    for tile in range(q_ref.shape[0] // TILE):
        for pick in range(TOPK):
            slot = slots_ref[0, (first_tile + tile) * TOPK + pick]
            owner, rank = slot >> 3, slot & (CAP - 1)
            away_x = ((owner >> 2) - my_x) & (SIDE - 1)
            away_y = ((owner & 3) - my_y) & (SIDE - 1)
            k_at = (away_y * SIDE + away_x) * CAP + rank
            v_at = (away_x * SIDE + away_y) * CAP + rank
            to = slice(pick * BLOCK, (pick + 1) * BLOCK)
            kt[tile % 2, to, :] = k_ref[pl.ds(pl.multiple_of(k_at * BLOCK, BLOCK), BLOCK), :]
            vt[tile % 2, to, :] = v_ref[pl.ds(pl.multiple_of(v_at * BLOCK, BLOCK), BLOCK), :]
        keys, values = kt[tile % 2], vt[tile % 2]
        rows = slice(tile * TILE, (tile + 1) * TILE)
        for head in range(GROUP):
            columns = slice(head * HEAD_DIM, (head + 1) * HEAD_DIM)
            scores = lax.dot_general(
                q_ref[rows, columns], keys, (((1,), (1,)), ((), ())),
                preferred_element_type=jnp.float32,
            ) * SCALE
            exponent = jnp.exp(scores - jnp.max(scores, axis=-1, keepdims=True))
            total = jnp.sum(exponent, axis=-1, keepdims=True)
            weights = (exponent * (1.0 / total)).astype(jnp.bfloat16)
            mixed = jnp.dot(weights, values, preferred_element_type=jnp.float32)
            o_ref[rows, columns] = mixed.astype(jnp.bfloat16)


def attend(first_tile, tiles, slots, place, queries, keys, values):
    width = queries.shape[1]
    rows = tiles * TILE
    return pl.pallas_call(
        functools.partial(attend_body, first_tile),
        in_specs=[SMEM_WHOLE, SMEM_WHOLE] + [VMEM_WHOLE] * 3,
        out_specs=VMEM_WHOLE,
        out_shape=jax.ShapeDtypeStruct((rows, width), jnp.bfloat16),
        scratch_shapes=[pltpu.VMEM((2, TOPK * BLOCK, HEAD_DIM), jnp.bfloat16)] * 2,
        compiler_params=pltpu.CompilerParams(vmem_limit_bytes=32 << 20),
        cost_estimate=pl.CostEstimate(
            flops=4 * rows * GROUP * TOPK * BLOCK * HEAD_DIM,
            bytes_accessed=4 * rows * width,
            transcendentals=rows * GROUP * TOPK * BLOCK,
        ),
        name="attend",
    )(slots, place, queries, keys, values)


def rms_normed(text_hidden, norm_gain):
    as_float = text_hidden.astype(jnp.float32)
    inverse = lax.rsqrt(jnp.mean(as_float * as_float, axis=-1, keepdims=True) + EPSILON)
    return (as_float * inverse * norm_gain).astype(jnp.bfloat16)


def spread(value, dx, dy):
    half = (value.shape[0] - NOTE_ROWS) // 2
    minus = along_seq(value, dx, dy)
    plus = along_seq(value, -dx, -dy)
    low = along_seq(minus[:half], dx, dy)
    high = along_seq(plus[half:], -dx, -dy)
    return plus, low, high, minus


def asks(own, plus, high, minus):
    rows = own.shape[0] - NOTE_ROWS
    at = high.shape[0] - NOTE_ROWS
    return jnp.concatenate(
        [own[rows : rows + 1], plus[rows : rows + 1], high[at : at + 1], minus[rows : rows + 1]]
    ).astype(jnp.int32)


def columns_of(weight, places):
    width = weight.shape[1] // 8
    return [lax.dynamic_slice_in_dim(weight, p * width, width, 1) for p in places]


def shards(
    text_hidden,
    norm_gain,
    image_features,
    query_weight,
    key_weight,
    value_weight,
    output_weight,
    selected,
):
    seq = lax.axis_index("seq")
    my_x, my_y = seq // SIDE, seq % SIDE
    section, z_hi = lax.axis_index("section"), lax.axis_index("head")
    z, core = z_hi * 2 + section // 2, section % 2

    k_own, v_own, slots = project(
        image_features, key_weight, value_weight, selected.reshape(1, PICKS)
    )
    k_plus, k_low, k_high, k_minus = spread(k_own, 1, 0)
    v_plus, v_low, v_high, v_minus = spread(v_own, 0, 1)

    def wanted_columns(z):
        return [
            column(z, core), column(3 - z, core), column(z, 1 - core), column(3 - z, 1 - core)
        ]

    own_weight = columns_of(output_weight, wanted_columns(z))
    near_weight = to_near(
        jnp.concatenate(columns_of(output_weight, wanted_columns(z ^ 1)), axis=1)
    )
    keep_own = jnp.concatenate(own_weight[:2], axis=1)
    give_own = jnp.concatenate(own_weight[2:], axis=1)
    kept = keep_own.shape[1]
    keep_near, give_near = near_weight[:, :kept], near_weight[:, kept:]

    normed = rms_normed(text_hidden, norm_gain)
    queries = jnp.dot(normed, query_weight, preferred_element_type=jnp.float32).astype(jnp.bfloat16)

    k_place = jnp.stack([my_x, my_y * CAP, SIDE * CAP + 0 * my_x])
    v_place = jnp.stack([my_y, my_x * (SIDE * CAP), CAP + 0 * my_y])
    k_out = pack(
        asks(v_own, v_plus, v_high, v_minus), k_place, k_own, k_plus, k_low, k_high, k_minus
    )
    v_out = pack(
        asks(k_own, k_plus, k_high, k_minus), v_place, v_own, v_plus, v_low, v_high, v_minus
    )
    keys = jnp.concatenate(
        [
            k_out[0],
            along_seq(k_out[3], 0, -1),
            along_seq(k_out[2], 0, 2),
            along_seq(k_out[1], 0, 1),
        ]
    )
    values = jnp.concatenate(
        [
            v_out[0],
            along_seq(v_out[3], -1, 0),
            along_seq(v_out[2], 2, 0),
            along_seq(v_out[1], 1, 0),
        ]
    )

    place = jnp.stack([my_x, my_y])
    tiles_dev = selected.shape[0]
    per = 2
    outs = []
    half = output_weight.shape[1] // 8

    def product(a, b):
        return jnp.dot(a, b, preferred_element_type=jnp.float32)

    for first in range(0, tiles_dev, per):
        rows = slice(first * TILE, (first + per) * TILE)
        mine = attend(first, per, slots, place, queries[rows], keys, values)
        near = to_near(mine)
        give = (product(mine, give_own) + product(near, give_near)).astype(jnp.bfloat16)
        got = to_core(give)
        keep = product(mine, keep_own) + product(near, keep_near)
        keep = keep + got.astype(jnp.float32)
        far = to_far(keep[:, half:].astype(jnp.bfloat16))
        outs.append((keep[:, :half] + far.astype(jnp.float32)).astype(jnp.bfloat16))
    return jnp.concatenate(outs, axis=0)


def solution(mesh):
    in_specs = (
        P("seq", None),
        P(),
        P("seq", None),
        P(None, ("section", "head")),
        P(None, ("section", "head")),
        P(None, ("section", "head")),
        P(("section", "head"), None),
        P("seq", None),
    )
    out_specs = P("seq", ("section", "head"))
    return jax.shard_map(shards, mesh=mesh, in_specs=in_specs, out_specs=out_specs, check_vma=False)
```

```python
import functools

import jax
import jax.numpy as jnp
from jax import lax
from jax.experimental import pallas as pl
from jax.experimental.pallas import tpu as pltpu
from jax.sharding import PartitionSpec as P

HEADS = 32
KV_HEADS = 8
HEAD_DIM = 128
GROUP = HEADS // KV_HEADS
TILE = 128
BLOCK = 64
TOPK = 16
SIDE = 4
CAP = 8
PICKS = SIDE * SIDE * CAP
NOTE_ROWS = 16
EPSILON = 1e-05
NEAR_PIECES = (128, 128, 192, 64)
CHUNKS = (2, 2, 2, 2)
AHEAD = 4
SCALE = HEAD_DIM**-0.5
LOG2_E = 1.4426950408889634

SECTION_HEAD = ("section", "head")
SMALL = pl.CostEstimate(flops=1, bytes_accessed=1, transcendentals=0)
VMEM_WHOLE = pl.BlockSpec(memory_space=pltpu.VMEM)
HBM_WHOLE = pl.BlockSpec(memory_space=pltpu.HBM)
SMEM_WHOLE = pl.BlockSpec(memory_space=pltpu.SMEM)


def along_seq(value, dx, dy):
    pairs = [
        (x * SIDE + y, (x + dx) % SIDE * SIDE + (y + dy) % SIDE)
        for x in range(SIDE)
        for y in range(SIDE)
    ]
    return lax.ppermute(value, "seq", pairs)


def column(z, core):
    return (z % 2) * 4 + core * 2 + z // 2


def along_z(value, place):
    pairs = []
    for z in range(4):
        for core in range(2):
            pairs.append((column(z, core), column(*place(z, core))))
    return lax.ppermute(value, SECTION_HEAD, pairs)


def to_near(value):
    return along_z(value, lambda z, core: (z ^ 1, core))


def to_far(value):
    return along_z(value, lambda z, core: (3 - z, core))


def to_core(value):
    return along_z(value, lambda z, core: (z, 1 - core))


def project_body(
    selected_ref, places_ref, x_ref, wk_ref, wv_ref, wo_ref, k_ref, v_ref, slots_ref, *rest
):
    piece_refs, (w_ref, sem) = rest[:-2], rest[-2:]
    step = pl.program_id(0)

    def copies():
        width = wo_ref.shape[1] // 8
        found, at = [], 0
        for index, piece in enumerate(piece_refs):
            for group in range(4):
                start = pl.multiple_of(places_ref[group] * width, width)
                found.append(
                    pltpu.make_async_copy(
                        wo_ref.at[pl.ds(at, piece.shape[0]), pl.ds(start, width)],
                        piece.at[:, pl.ds(group * width, width)],
                        sem.at[index * 4 + group],
                    )
                )
            at += piece.shape[0]
        return found

    rows = x_ref.shape[0]
    steps = pl.num_programs(0)
    blocks_dev = (k_ref.shape[0] - NOTE_ROWS) // BLOCK
    blocks = SIDE * SIDE * blocks_dev

    @pl.when(step == 0)
    def _():
        w_ref[:, :HEAD_DIM] = wk_ref[...]
        w_ref[:, HEAD_DIM:] = wv_ref[...]
        for copy in copies():
            copy.start()

    @pl.when(step == steps - 1)
    def _():
        picked = selected_ref[...]
        tiles, per_tile = picked.shape
        source = lax.broadcasted_iota(jnp.int32, (per_tile, PICKS), 0)
        place = lax.broadcasted_iota(jnp.int32, (per_tile, PICKS), 1)
        repeat = (place % per_tile == source).astype(jnp.float32).astype(jnp.bfloat16)

        def repeated(part):
            part = part.astype(jnp.float32).astype(jnp.bfloat16)
            return jnp.dot(part, repeat, preferred_element_type=jnp.float32)

        wide = repeated(picked // blocks_dev) * blocks_dev + repeated(picked % blocks_dev)
        tile = lax.broadcasted_iota(jnp.int32, (tiles, PICKS), 0)
        at = lax.broadcasted_iota(jnp.int32, (tiles, PICKS), 1)
        ids = jnp.sum(jnp.where(at // per_tile == tile, wide, 0.0), axis=0, keepdims=True)

        block = lax.broadcasted_iota(jnp.int32, (blocks, PICKS), 0)
        hit = (block == ids.astype(jnp.int32)).astype(jnp.float32)
        wanted = jnp.broadcast_to(jnp.max(hit, axis=1, keepdims=True), (blocks, PICKS))
        one = lax.broadcasted_iota(jnp.int32, (blocks, blocks), 0)
        other = lax.broadcasted_iota(jnp.int32, (blocks, blocks), 1)
        before = (one // blocks_dev == other // blocks_dev) & (other < one)
        rank = jnp.dot(
            before.astype(jnp.float32).astype(jnp.bfloat16),
            wanted.astype(jnp.bfloat16),
            preferred_element_type=jnp.float32,
        )
        owner = block // blocks_dev
        slot = (owner * CAP).astype(jnp.float32) + rank
        slots = jnp.sum(hit * slot, axis=0, keepdims=True)
        slots_ref[...] = jnp.broadcast_to(slots, slots_ref.shape).astype(jnp.int32)
        place = lax.broadcasted_iota(jnp.int32, (blocks, PICKS), 1).astype(jnp.float32)
        local = (block % blocks_dev).astype(jnp.float32)
        asked = jnp.sum(
            jnp.where(slot == place, wanted * local, 0.0), axis=0, keepdims=True
        )
        note = jnp.broadcast_to(asked, (NOTE_ROWS, PICKS)).astype(jnp.bfloat16)
        k_ref[rows * steps :, :] = note
        v_ref[rows * steps :, :] = note

    both = jnp.dot(x_ref[...], w_ref[...], preferred_element_type=jnp.float32)
    at = pl.ds(pl.multiple_of(step * rows, rows), rows)
    k_ref[at, :] = both[:, :HEAD_DIM].astype(jnp.bfloat16)
    v_ref[at, :] = both[:, HEAD_DIM:].astype(jnp.bfloat16)

    @pl.when(step == steps - 1)
    def _():
        for copy in copies():
            copy.wait()


def in_hbm(value):
    return pltpu.with_memory_space_constraint(value, pltpu.HBM)


def project(image_features, key_weight, value_weight, selected, places, output_weight):
    rows, enc = image_features.shape
    steps = 4
    out = jax.ShapeDtypeStruct((rows + NOTE_ROWS, HEAD_DIM), jnp.bfloat16)
    whole = lambda shape: pl.BlockSpec(shape, lambda i: (0,) * len(shape))
    return pl.pallas_call(
        project_body,
        grid=(steps,),
        in_specs=[
            whole(selected.shape),
            SMEM_WHOLE,
            pl.BlockSpec((rows // steps, enc), lambda i: (i, 0)),
            whole((enc, HEAD_DIM)),
            whole((enc, HEAD_DIM)),
            HBM_WHOLE,
        ],
        out_specs=[
            whole((rows + NOTE_ROWS, HEAD_DIM)),
            whole((rows + NOTE_ROWS, HEAD_DIM)),
            whole((8, PICKS)),
            *[HBM_WHOLE for _ in NEAR_PIECES],
        ],
        out_shape=[
            out,
            out,
            jax.ShapeDtypeStruct((8, PICKS), jnp.int32),
            *[
                jax.ShapeDtypeStruct((rows, output_weight.shape[1] // 2), output_weight.dtype)
                for rows in NEAR_PIECES
            ],
        ],
        scratch_shapes=[
            pltpu.VMEM((enc, 2 * HEAD_DIM), jnp.bfloat16),
            pltpu.SemaphoreType.DMA((4 * len(NEAR_PIECES),)),
        ],
        compiler_params=pltpu.CompilerParams(vmem_limit_bytes=40 << 20),
        cost_estimate=SMALL,
        name="project",
    )(
        selected,
        places,
        in_hbm(image_features),
        in_hbm(key_weight),
        in_hbm(value_weight),
        in_hbm(output_weight),
    )


def pack_one(ask, me, base, stride, own, plus, two, minus, here, up, down):
    chunk = SIDE * CAP * BLOCK

    def rows(ref, index):
        return ref[pl.ds(pl.multiple_of(index * BLOCK, BLOCK), BLOCK), :]

    for dest in range(SIDE):
        for away in range(SIDE):
            first = base + ((me + away) & (SIDE - 1)) * stride
            for slot in range(CAP):
                block = ask[dest, first + slot]
                value = rows((own, plus, two, minus)[away], block)
                at = (away * CAP + slot) * BLOCK
                if dest == 0:
                    here[at : at + BLOCK, :] = value
                elif dest == 1:
                    up[at : at + BLOCK, :] = value
                elif dest == 3:
                    down[at : at + BLOCK, :] = value
                elif at < chunk // 2:
                    up[chunk + at : chunk + at + BLOCK, :] = value
                else:
                    down[chunk // 2 + at : chunk // 2 + at + BLOCK, :] = value


def pack_body(place_ref, *refs):
    k_in, v_in, k_out, v_out = refs[:4], refs[4:8], refs[8:11], refs[11:14]
    note_ref, ask_ref, sem = refs[14:]

    def note(ring):
        last = lambda ref: ref[ref.shape[0] - NOTE_ROWS :, :].astype(jnp.float32)[:1]
        return jnp.concatenate([last(ref) for ref in ring], axis=0)

    notes = jnp.concatenate([note(v_in), note(k_in)], axis=0)
    note_ref[...] = notes.astype(jnp.int32)
    copy = pltpu.make_async_copy(note_ref, ask_ref, sem)
    copy.start()
    copy.wait()
    my_x, my_y = place_ref[0], place_ref[1]
    pack_one(ask_ref, my_x, my_y * CAP, SIDE * CAP, *k_in, *k_out)
    pack_one(ask_ref.at[SIDE:], my_y, my_x * (SIDE * CAP), CAP, *v_in, *v_out)


def pack(place, k_in, v_in):
    chunk = SIDE * CAP * BLOCK
    outs = [
        jax.ShapeDtypeStruct((rows, HEAD_DIM), jnp.bfloat16)
        for rows in (chunk, chunk + chunk // 2, chunk + chunk // 2)
    ]
    out = pl.pallas_call(
        pack_body,
        in_specs=[SMEM_WHOLE] + [VMEM_WHOLE] * 8,
        out_specs=[VMEM_WHOLE] * 6,
        out_shape=outs + outs,
        scratch_shapes=[
            pltpu.VMEM((2 * SIDE, PICKS), jnp.int32),
            pltpu.SMEM((2 * SIDE, PICKS), jnp.int32),
            pltpu.SemaphoreType.DMA,
        ],
        compiler_params=pltpu.CompilerParams(vmem_limit_bytes=32 << 20),
        cost_estimate=SMALL,
        name="pack",
    )(place, *k_in, *v_in)
    return out[:3], out[3:]


def attend_body(first_tile, slots_ref, place_ref, q_ref, k_ref, v_ref, o_ref, kt, vt):
    my_x, my_y = place_ref[0], place_ref[1]
    for tile in range(o_ref.shape[0] // TILE):
        for pick in range(TOPK):
            slot = slots_ref[0, (first_tile + tile) * TOPK + pick]
            owner, rank = slot >> 3, slot & (CAP - 1)
            away_x = ((owner >> 2) - my_x) & (SIDE - 1)
            away_y = ((owner & 3) - my_y) & (SIDE - 1)
            k_at = (away_y * SIDE + away_x) * CAP + rank
            v_at = (away_x * SIDE + away_y) * CAP + rank
            to = slice(pick * BLOCK, (pick + 1) * BLOCK)
            kt[tile % 2, to, :] = k_ref[pl.ds(pl.multiple_of(k_at * BLOCK, BLOCK), BLOCK), :]
            vt[tile % 2, to, :] = v_ref[pl.ds(pl.multiple_of(v_at * BLOCK, BLOCK), BLOCK), :]
        rows = slice(tile * TILE, (tile + 1) * TILE)
        asking = slice((first_tile + tile) * TILE, (first_tile + tile + 1) * TILE)
        heads = [slice(h * HEAD_DIM, (h + 1) * HEAD_DIM) for h in range(GROUP)]
        stacked = jnp.concatenate([q_ref[asking, columns] for columns in heads], axis=0)
        scores = lax.dot_general(
            stacked, kt[tile % 2], (((1,), (1,)), ((), ())), preferred_element_type=jnp.float32
        )
        largest = jnp.max(scores, axis=-1, keepdims=True)
        exponent = jnp.exp2((scores - largest) * (SCALE * LOG2_E))
        total = jnp.sum(exponent, axis=-1, keepdims=True)
        weights = (exponent * (1.0 / total)).astype(jnp.bfloat16)
        mixed = jnp.dot(weights, vt[tile % 2], preferred_element_type=jnp.float32)
        mixed = mixed.astype(jnp.bfloat16)
        for h, columns in enumerate(heads):
            o_ref[rows, columns] = mixed[h * TILE : (h + 1) * TILE]


def attend(first_tile, tiles, slots, place, queries, keys, values):
    width = queries.shape[1]
    rows = tiles * TILE
    return pl.pallas_call(
        functools.partial(attend_body, first_tile),
        in_specs=[SMEM_WHOLE, SMEM_WHOLE] + [VMEM_WHOLE] * 3,
        out_specs=VMEM_WHOLE,
        out_shape=jax.ShapeDtypeStruct((rows, width), jnp.bfloat16),
        scratch_shapes=[pltpu.VMEM((2, TOPK * BLOCK, HEAD_DIM), jnp.bfloat16)] * 2,
        compiler_params=pltpu.CompilerParams(vmem_limit_bytes=32 << 20),
        cost_estimate=SMALL,
        name="attend",
    )(slots, place, queries, keys, values)


def pick_body(places_ref, w_ref, *out_refs):
    at = 0
    for ref in out_refs:
        ref[...] = w_ref[at : at + ref.shape[0], :]
        at += ref.shape[0]


def pick(places, weight, pieces):
    depth, width = weight.shape[0], weight.shape[1] // 8
    return pl.pallas_call(
        pick_body,
        grid_spec=pltpu.PrefetchScalarGridSpec(
            num_scalar_prefetch=1,
            grid=(4,),
            in_specs=[pl.BlockSpec((depth, width), lambda i, places: (0, places[i]))],
            out_specs=[pl.BlockSpec((rows, width), lambda i, places: (0, i)) for rows in pieces],
        ),
        out_shape=[jax.ShapeDtypeStruct((rows, 4 * width), weight.dtype) for rows in pieces],
        compiler_params=pltpu.CompilerParams(vmem_limit_bytes=8 << 20),
        cost_estimate=SMALL,
        name="pick",
    )(places, in_hbm(weight))


def multiply_body(mine_ref, near_ref, w_ref, *out_refs):
    left = jnp.concatenate([mine_ref[...], near_ref[...]], axis=1)
    width = w_ref.shape[1] // len(out_refs)
    for group, out_ref in enumerate(out_refs):
        columns = slice(group * width, (group + 1) * width)
        product = jnp.dot(left, w_ref[:, columns], preferred_element_type=jnp.float32)
        out_ref[...] = product.astype(out_ref.dtype)


def multiply(mine, near, weight):
    shape = (mine.shape[0], weight.shape[1] // 4)
    give = jax.ShapeDtypeStruct(shape, jnp.bfloat16)
    keep = jax.ShapeDtypeStruct(shape, jnp.float32)
    return pl.pallas_call(
        multiply_body,
        in_specs=[VMEM_WHOLE] * 3,
        out_specs=[VMEM_WHOLE] * 4,
        out_shape=[give, give, keep, keep],
        compiler_params=pltpu.CompilerParams(vmem_limit_bytes=24 << 20),
        cost_estimate=SMALL,
        name="multiply",
    )(mine, near, weight)


def rms_normed(text_hidden, norm_gain):
    as_float = text_hidden.astype(jnp.float32)
    inverse = lax.rsqrt(jnp.mean(as_float * as_float, axis=-1, keepdims=True) + EPSILON)
    return (as_float * inverse * norm_gain).astype(jnp.bfloat16)


def after(value, other):
    return lax.optimization_barrier((value, other))[0]


def spread(value, dx, dy, hold=lambda part: part):
    minus = along_seq(value, dx, dy)
    plus = along_seq(value, -dx, -dy)
    return value, plus, along_seq(hold(minus), dx, dy), minus


def exchange(packed, dx, dy, hold=lambda part: part):
    here, up, down = packed
    chunk = here.shape[0]
    minus = along_seq(up, dx, dy)
    plus = along_seq(down, -dx, -dy)
    low = along_seq(minus[chunk:], dx, dy)
    high = along_seq(hold(plus)[chunk:], -dx, -dy)
    return jnp.concatenate([here, plus[:chunk], low, high, minus[:chunk]])


def shards(
    text_hidden,
    norm_gain,
    image_features,
    query_weight,
    key_weight,
    value_weight,
    output_weight,
    selected,
):
    seq = lax.axis_index("seq")
    my_x, my_y = seq // SIDE, seq % SIDE
    section, z_hi = lax.axis_index("section"), lax.axis_index("head")
    z, core = z_hi * 2 + section // 2, section % 2

    place = jnp.stack([my_x, my_y])

    def wanted_columns(z):
        return jnp.stack(
            [column(3 - z, 1 - core), column(z, 1 - core), column(3 - z, core), column(z, core)]
        )

    k_own, v_own, slots, *pieces = project(
        image_features, key_weight, value_weight, selected, wanted_columns(z ^ 1), output_weight
    )
    near_weight = [to_near(piece) for piece in pieces]
    k_ring = spread(k_own, 1, 0)
    v_ring = spread(v_own, 0, 1, lambda part: after(part, near_weight[0]))
    k_out, v_out = pack(after(place, near_weight[1]), k_ring, v_ring)
    keys = exchange(k_out, 0, 1)
    values = exchange(v_out, 1, 0, lambda part: after(part, near_weight[2]))

    text_hidden = after(text_hidden, k_out[0])
    normed = rms_normed(text_hidden, norm_gain)
    queries = jnp.dot(normed, query_weight, preferred_element_type=jnp.float32).astype(jnp.bfloat16)
    own_weight = pick(
        wanted_columns(z), after(output_weight, k_out[0]), (output_weight.shape[0],)
    )
    weight = jnp.concatenate([*own_weight, *near_weight])

    starts = [sum(CHUNKS[:index]) for index in range(len(CHUNKS))]
    mine, near, sent, outs = [], [], [], []

    def attended(slots):
        index = len(mine)
        part = attend(starts[index], CHUNKS[index], slots, place, queries, keys, values)
        mine.append(part)
        near.append(to_near(part))
        return after(slots, part)

    while len(mine) < AHEAD:
        slots = attended(slots)
    weight = after(weight, mine[-1])
    last = len(CHUNKS) - 1
    for index in range(len(CHUNKS)):
        if index >= 2:
            weight = after(weight, sent[index - 2])
        if index >= 3:
            weight = after(weight, outs[index - 3])
        give_far, give_own, keep_far, keep_own = multiply(mine[index], near[index], weight)
        weight = after(weight, give_far)
        if len(mine) < len(CHUNKS):
            slots = attended(after(slots, give_far))
            weight = after(weight, mine[-1])
        got_far, got_own = to_core(give_far), to_core(give_own)
        if index >= 2 and index == last:
            got_far = after(got_far, outs[index - 2])
        send = (keep_far + got_far.astype(jnp.float32)).astype(jnp.bfloat16)
        far = to_far(send)
        sent.append(send)
        total = keep_own + got_own.astype(jnp.float32) + far.astype(jnp.float32)
        outs.append(total.astype(jnp.bfloat16))
    return jnp.concatenate(outs, axis=0)


def solution(mesh):
    in_specs = (
        P("seq", None),
        P(),
        P("seq", None),
        P(None, ("section", "head")),
        P(None, ("section", "head")),
        P(None, ("section", "head")),
        P(("section", "head"), None),
        P("seq", None),
    )
    out_specs = P("seq", ("section", "head"))
    return jax.shard_map(shards, mesh=mesh, in_specs=in_specs, out_specs=out_specs, check_vma=False)
```

```python
import functools

import jax
import jax.numpy as jnp
from jax import lax
from jax.experimental import pallas as pl
from jax.experimental.pallas import tpu as pltpu
from jax.sharding import PartitionSpec as P

HEADS = 32
KV_HEADS = 8
HEAD_DIM = 128
GROUP = HEADS // KV_HEADS
TILE = 128
BLOCK = 64
TOPK = 16
SIDE = 4
CAP = 8
PICKS = SIDE * SIDE * CAP
NOTE_ROWS = 16
EPSILON = 1e-05
NEAR_PIECES = (128, 128, 128, 128)
CHUNKS = (2, 2, 2, 2)
AHEAD = 3
SCALE = HEAD_DIM**-0.5
LOG2_E = 1.4426950408889634

SECTION_HEAD = ("section", "head")
SMALL = pl.CostEstimate(flops=1, bytes_accessed=1, transcendentals=0)
VMEM_WHOLE = pl.BlockSpec(memory_space=pltpu.VMEM)
SMEM_WHOLE = pl.BlockSpec(memory_space=pltpu.SMEM)


def along_seq(value, dx, dy):
    pairs = [
        (x * SIDE + y, (x + dx) % SIDE * SIDE + (y + dy) % SIDE)
        for x in range(SIDE)
        for y in range(SIDE)
    ]
    return lax.ppermute(value, "seq", pairs)


def column(z, core):
    return (z % 2) * 4 + core * 2 + z // 2


def along_z(value, place):
    pairs = []
    for z in range(4):
        for core in range(2):
            pairs.append((column(z, core), column(*place(z, core))))
    return lax.ppermute(value, SECTION_HEAD, pairs)


def to_near(value):
    return along_z(value, lambda z, core: (z ^ 1, core))


def to_far(value):
    return along_z(value, lambda z, core: (3 - z, core))


def to_core(value):
    return along_z(value, lambda z, core: (z, 1 - core))


def project_body(
    places_ref, selected_ref, x_ref, wk_ref, wv_ref, wo_ref, k_ref, v_ref, slots_ref, *rest
):
    piece_refs, w_ref = rest[:-1], rest[-1]
    step = pl.program_id(0)

    at = 0
    for piece in piece_refs:
        piece[...] = wo_ref[at : at + piece.shape[0], :]
        at += piece.shape[0]

    rows = x_ref.shape[0]
    steps = pl.num_programs(0)
    blocks_dev = (k_ref.shape[0] - NOTE_ROWS) // BLOCK
    blocks = SIDE * SIDE * blocks_dev

    @pl.when(step == 0)
    def _():
        w_ref[:, :HEAD_DIM] = wk_ref[...]
        w_ref[:, HEAD_DIM:] = wv_ref[...]
    @pl.when(step == steps - 1)
    def _():
        picked = selected_ref[...]
        tiles, per_tile = picked.shape
        source = lax.broadcasted_iota(jnp.int32, (per_tile, PICKS), 0)
        place = lax.broadcasted_iota(jnp.int32, (per_tile, PICKS), 1)
        repeat = (place % per_tile == source).astype(jnp.float32).astype(jnp.bfloat16)

        def repeated(part):
            part = part.astype(jnp.float32).astype(jnp.bfloat16)
            return jnp.dot(part, repeat, preferred_element_type=jnp.float32)

        wide = repeated(picked // blocks_dev) * blocks_dev + repeated(picked % blocks_dev)
        tile = lax.broadcasted_iota(jnp.int32, (tiles, PICKS), 0)
        at = lax.broadcasted_iota(jnp.int32, (tiles, PICKS), 1)
        ids = jnp.sum(jnp.where(at // per_tile == tile, wide, 0.0), axis=0, keepdims=True)

        block = lax.broadcasted_iota(jnp.int32, (blocks, PICKS), 0)
        hit = (block == ids.astype(jnp.int32)).astype(jnp.float32)
        wanted = jnp.broadcast_to(jnp.max(hit, axis=1, keepdims=True), (blocks, PICKS))
        one = lax.broadcasted_iota(jnp.int32, (blocks, blocks), 0)
        other = lax.broadcasted_iota(jnp.int32, (blocks, blocks), 1)
        before = (one // blocks_dev == other // blocks_dev) & (other < one)
        rank = jnp.dot(
            before.astype(jnp.float32).astype(jnp.bfloat16),
            wanted.astype(jnp.bfloat16),
            preferred_element_type=jnp.float32,
        )
        owner = block // blocks_dev
        slot = (owner * CAP).astype(jnp.float32) + rank
        slots = jnp.sum(hit * slot, axis=0, keepdims=True)
        slots_ref[...] = jnp.broadcast_to(slots, slots_ref.shape).astype(jnp.int32)
        place = lax.broadcasted_iota(jnp.int32, (blocks, PICKS), 1).astype(jnp.float32)
        local = (block % blocks_dev).astype(jnp.float32)
        asked = jnp.sum(
            jnp.where(slot == place, wanted * local, 0.0), axis=0, keepdims=True
        )
        note = jnp.broadcast_to(asked, (NOTE_ROWS, PICKS)).astype(jnp.bfloat16)
        k_ref[rows * steps :, :] = note
        v_ref[rows * steps :, :] = note

    both = jnp.dot(x_ref[...], w_ref[...], preferred_element_type=jnp.float32)
    at = pl.ds(pl.multiple_of(step * rows, rows), rows)
    k_ref[at, :] = both[:, :HEAD_DIM].astype(jnp.bfloat16)
    v_ref[at, :] = both[:, HEAD_DIM:].astype(jnp.bfloat16)


def in_hbm(value):
    return pltpu.with_memory_space_constraint(value, pltpu.HBM)


def project(image_features, key_weight, value_weight, selected, places, output_weight):
    rows, enc = image_features.shape
    steps = 4
    out = jax.ShapeDtypeStruct((rows + NOTE_ROWS, HEAD_DIM), jnp.bfloat16)
    whole = lambda shape: pl.BlockSpec(shape, lambda i, places: (0,) * len(shape))
    depth, width = output_weight.shape[0], output_weight.shape[1] // 8
    return pl.pallas_call(
        project_body,
        grid_spec=pltpu.PrefetchScalarGridSpec(
            num_scalar_prefetch=1,
            grid=(steps,),
            in_specs=[
                whole(selected.shape),
                pl.BlockSpec((rows // steps, enc), lambda i, places: (i, 0)),
                whole((enc, HEAD_DIM)),
                whole((enc, HEAD_DIM)),
                pl.BlockSpec((depth, width), lambda i, places: (0, places[i])),
            ],
            out_specs=[
                whole((rows + NOTE_ROWS, HEAD_DIM)),
                whole((rows + NOTE_ROWS, HEAD_DIM)),
                whole((8, PICKS)),
                *[pl.BlockSpec((part, width), lambda i, places: (0, i)) for part in NEAR_PIECES],
            ],
            scratch_shapes=[pltpu.VMEM((enc, 2 * HEAD_DIM), jnp.bfloat16)],
        ),
        out_shape=[
            out,
            out,
            jax.ShapeDtypeStruct((8, PICKS), jnp.int32),
            *[
                jax.ShapeDtypeStruct((part, steps * width), output_weight.dtype)
                for part in NEAR_PIECES
            ],
        ],
        compiler_params=pltpu.CompilerParams(vmem_limit_bytes=40 << 20),
        cost_estimate=SMALL,
        name="project",
    )(
        places,
        selected,
        in_hbm(image_features),
        in_hbm(key_weight),
        in_hbm(value_weight),
        in_hbm(output_weight),
    )


def pack_one(ask, me, base, stride, ring, outs):
    for dest, out in enumerate(outs):
        for away, ref in enumerate(ring):
            first = base + ((me + away) & (SIDE - 1)) * stride
            for slot in range(CAP):
                block = pl.multiple_of(ask[dest, first + slot] * BLOCK, BLOCK)
                at = (away * CAP + slot) * BLOCK
                out[at : at + BLOCK, :] = ref[pl.ds(block, BLOCK), :]


def pack_body(place_ref, *refs):
    k_in, v_in, k_out, v_out = refs[:4], refs[4:8], refs[8:12], refs[12:16]
    note_ref, ask_ref, sem = refs[16:]

    def note(ring):
        last = lambda ref: ref[ref.shape[0] - NOTE_ROWS :, :].astype(jnp.float32)[:1]
        return jnp.concatenate([last(ref) for ref in ring], axis=0)

    notes = jnp.concatenate([note(v_in), note(k_in)], axis=0)
    note_ref[...] = notes.astype(jnp.int32)
    copy = pltpu.make_async_copy(note_ref, ask_ref, sem)
    copy.start()
    copy.wait()
    my_x, my_y = place_ref[0], place_ref[1]
    pack_one(ask_ref, my_x, my_y * CAP, SIDE * CAP, k_in, k_out)
    pack_one(ask_ref.at[SIDE:], my_y, my_x * (SIDE * CAP), CAP, v_in, v_out)


def pack(place, k_in, v_in):
    outs = [jax.ShapeDtypeStruct((SIDE * CAP * BLOCK, HEAD_DIM), jnp.bfloat16)] * SIDE
    out = pl.pallas_call(
        pack_body,
        in_specs=[SMEM_WHOLE] + [VMEM_WHOLE] * 8,
        out_specs=[VMEM_WHOLE] * 8,
        out_shape=outs + outs,
        scratch_shapes=[
            pltpu.VMEM((2 * SIDE, PICKS), jnp.int32),
            pltpu.SMEM((2 * SIDE, PICKS), jnp.int32),
            pltpu.SemaphoreType.DMA,
        ],
        compiler_params=pltpu.CompilerParams(vmem_limit_bytes=32 << 20),
        cost_estimate=SMALL,
        name="pack",
    )(place, *k_in, *v_in)
    return out[:4], out[4:]


def attend_body(first_tile, slots_ref, place_ref, q_ref, k_ref, v_ref, o_ref, kt, vt):
    my_x, my_y = place_ref[0], place_ref[1]
    for tile in range(o_ref.shape[0] // TILE):
        for pick in range(TOPK):
            slot = slots_ref[0, (first_tile + tile) * TOPK + pick]
            owner, rank = slot >> 3, slot & (CAP - 1)
            away_x = ((owner >> 2) - my_x) & (SIDE - 1)
            away_y = ((owner & 3) - my_y) & (SIDE - 1)
            k_at = (away_y * SIDE + away_x) * CAP + rank
            v_at = (away_x * SIDE + away_y) * CAP + rank
            to = slice(pick * BLOCK, (pick + 1) * BLOCK)
            kt[tile % 2, to, :] = k_ref[pl.ds(pl.multiple_of(k_at * BLOCK, BLOCK), BLOCK), :]
            vt[tile % 2, to, :] = v_ref[pl.ds(pl.multiple_of(v_at * BLOCK, BLOCK), BLOCK), :]
        rows = slice(tile * TILE, (tile + 1) * TILE)
        asking = slice((first_tile + tile) * TILE, (first_tile + tile + 1) * TILE)
        heads = [slice(h * HEAD_DIM, (h + 1) * HEAD_DIM) for h in range(GROUP)]
        stacked = jnp.concatenate([q_ref[asking, columns] for columns in heads], axis=0)
        scores = lax.dot_general(
            stacked, kt[tile % 2], (((1,), (1,)), ((), ())), preferred_element_type=jnp.float32
        )
        largest = jnp.max(scores, axis=-1, keepdims=True)
        exponent = jnp.exp2((scores - largest) * (SCALE * LOG2_E))
        total = jnp.sum(exponent, axis=-1, keepdims=True)
        weights = (exponent * (1.0 / total)).astype(jnp.bfloat16)
        mixed = jnp.dot(weights, vt[tile % 2], preferred_element_type=jnp.float32)
        mixed = mixed.astype(jnp.bfloat16)
        for h, columns in enumerate(heads):
            o_ref[rows, columns] = mixed[h * TILE : (h + 1) * TILE]


def attend(first_tile, tiles, slots, place, queries, keys, values):
    width = queries.shape[1]
    rows = tiles * TILE
    return pl.pallas_call(
        functools.partial(attend_body, first_tile),
        in_specs=[SMEM_WHOLE, SMEM_WHOLE] + [VMEM_WHOLE] * 3,
        out_specs=VMEM_WHOLE,
        out_shape=jax.ShapeDtypeStruct((rows, width), jnp.bfloat16),
        scratch_shapes=[pltpu.VMEM((2, TOPK * BLOCK, HEAD_DIM), jnp.bfloat16)] * 2,
        compiler_params=pltpu.CompilerParams(vmem_limit_bytes=32 << 20),
        cost_estimate=SMALL,
        name="attend",
    )(slots, place, queries, keys, values)


def pick_body(places_ref, w_ref, *out_refs):
    at = 0
    for ref in out_refs:
        ref[...] = w_ref[at : at + ref.shape[0], :]
        at += ref.shape[0]


def pick(places, weight, pieces):
    depth, width = weight.shape[0], weight.shape[1] // 8
    return pl.pallas_call(
        pick_body,
        grid_spec=pltpu.PrefetchScalarGridSpec(
            num_scalar_prefetch=1,
            grid=(4,),
            in_specs=[pl.BlockSpec((depth, width), lambda i, places: (0, places[i]))],
            out_specs=[pl.BlockSpec((rows, width), lambda i, places: (0, i)) for rows in pieces],
        ),
        out_shape=[jax.ShapeDtypeStruct((rows, 4 * width), weight.dtype) for rows in pieces],
        compiler_params=pltpu.CompilerParams(vmem_limit_bytes=8 << 20),
        cost_estimate=SMALL,
        name="pick",
    )(places, in_hbm(weight))


def multiply_body(mine_ref, near_ref, w_ref, *out_refs):
    left = jnp.concatenate([mine_ref[...], near_ref[...]], axis=1)
    width = w_ref.shape[1] // len(out_refs)
    for group, out_ref in enumerate(out_refs):
        columns = slice(group * width, (group + 1) * width)
        product = jnp.dot(left, w_ref[:, columns], preferred_element_type=jnp.float32)
        out_ref[...] = product.astype(out_ref.dtype)


def multiply(mine, near, weight):
    shape = (mine.shape[0], weight.shape[1] // 4)
    give = jax.ShapeDtypeStruct(shape, jnp.bfloat16)
    keep = jax.ShapeDtypeStruct(shape, jnp.float32)
    return pl.pallas_call(
        multiply_body,
        in_specs=[VMEM_WHOLE] * 3,
        out_specs=[VMEM_WHOLE] * 4,
        out_shape=[give, give, keep, keep],
        compiler_params=pltpu.CompilerParams(vmem_limit_bytes=24 << 20),
        cost_estimate=SMALL,
        name="multiply",
    )(mine, near, weight)


def rms_normed(text_hidden, norm_gain):
    as_float = text_hidden.astype(jnp.float32)
    inverse = lax.rsqrt(jnp.mean(as_float * as_float, axis=-1, keepdims=True) + EPSILON)
    return (as_float * inverse * norm_gain).astype(jnp.bfloat16)


def after(value, other):
    return lax.optimization_barrier((value, other))[0]


def spread(value, dx, dy, hold=lambda part: part):
    minus = along_seq(value, dx, dy)
    plus = along_seq(value, -dx, -dy)
    two = along_seq(hold(after(value, minus)), 2 * dx, 2 * dy)
    return value, plus, two, minus


def exchange(packed, dx, dy, hold=lambda part: part):
    here, up, across, down = packed
    minus = along_seq(up, dx, dy)
    plus = along_seq(down, -dx, -dy)
    two = along_seq(hold(after(across, minus)), 2 * dx, 2 * dy)
    return jnp.concatenate([here, plus, two, minus])


def shards(
    text_hidden,
    norm_gain,
    image_features,
    query_weight,
    key_weight,
    value_weight,
    output_weight,
    selected,
):
    seq = lax.axis_index("seq")
    my_x, my_y = seq // SIDE, seq % SIDE
    section, z_hi = lax.axis_index("section"), lax.axis_index("head")
    z, core = z_hi * 2 + section // 2, section % 2

    place = jnp.stack([my_x, my_y])

    def wanted_columns(z):
        return jnp.stack(
            [column(3 - z, 1 - core), column(z, 1 - core), column(3 - z, core), column(z, core)]
        )

    k_own, v_own, slots, *pieces = project(
        image_features, key_weight, value_weight, selected, wanted_columns(z ^ 1), output_weight
    )
    near_weight = []
    for piece in pieces:
        near_weight.append(to_near(after(piece, near_weight[-1]) if near_weight else piece))
    k_ring = spread(k_own, 1, 0)
    v_ring = spread(v_own, 0, 1, lambda part: after(part, near_weight[0]))

    normed = rms_normed(after(text_hidden, k_own), norm_gain)
    queries = jnp.dot(normed, query_weight, preferred_element_type=jnp.float32).astype(jnp.bfloat16)

    k_out, v_out = pack(after(after(place, near_weight[1]), queries), k_ring, v_ring)
    keys = exchange(k_out, 0, 1)
    values = exchange(v_out, 1, 0, lambda part: after(part, near_weight[2]))
    own_weight = pick(
        wanted_columns(z), after(output_weight, k_out[0]), (output_weight.shape[0],)
    )
    weight = jnp.concatenate([*own_weight, *near_weight])

    starts = [sum(CHUNKS[:index]) for index in range(len(CHUNKS))]
    mine, near, sent, outs = [], [], [], []

    def attended(slots):
        index = len(mine)
        part = attend(starts[index], CHUNKS[index], slots, place, queries, keys, values)
        mine.append(part)
        near.append(to_near(part))
        return after(slots, part)

    while len(mine) < AHEAD:
        slots = attended(slots)
    weight = after(weight, mine[-1])
    last = len(CHUNKS) - 1
    for index in range(len(CHUNKS)):
        if index >= 2:
            weight = after(weight, sent[index - 2])
        if index >= 3:
            weight = after(weight, outs[index - 3])
        give_far, give_own, keep_far, keep_own = multiply(mine[index], near[index], weight)
        weight = after(weight, give_far)
        if len(mine) < len(CHUNKS):
            slots = attended(after(slots, give_far))
            weight = after(weight, mine[-1])
        got_far, got_own = to_core(give_far), to_core(give_own)
        if index >= 2 and index == last:
            got_far = after(got_far, outs[index - 2])
        send = (keep_far + got_far.astype(jnp.float32)).astype(jnp.bfloat16)
        far = to_far(send)
        sent.append(send)
        total = keep_own + got_own.astype(jnp.float32) + far.astype(jnp.float32)
        outs.append(total.astype(jnp.bfloat16))
    return jnp.concatenate(outs, axis=0)


def solution(mesh):
    in_specs = (
        P("seq", None),
        P(),
        P("seq", None),
        P(None, ("section", "head")),
        P(None, ("section", "head")),
        P(None, ("section", "head")),
        P(("section", "head"), None),
        P("seq", None),
    )
    out_specs = P("seq", ("section", "head"))
    return jax.shard_map(shards, mesh=mesh, in_specs=in_specs, out_specs=out_specs, check_vma=False)
```

```python
import functools

import jax
import jax.numpy as jnp
from jax import lax
from jax.experimental import pallas as pl
from jax.experimental.pallas import tpu as pltpu
from jax.sharding import PartitionSpec as P

HEADS = 32
KV_HEADS = 8
HEAD_DIM = 128
GROUP = HEADS // KV_HEADS
TILE = 128
BLOCK = 64
TOPK = 16
SIDE = 4
CAP = 8
PICKS = SIDE * SIDE * CAP
NOTE_ROWS = 16
EPSILON = 1e-05
NEAR_PIECES = (160, 192, 160)
CHUNKS = (2, 2, 2, 2)
AHEAD = 3
LAG = 2
FIN = 3
GOT = 2
SCALE = HEAD_DIM**-0.5
LOG2_E = 1.4426950408889634

SECTION_HEAD = ("section", "head")
SMALL = pl.CostEstimate(flops=1, bytes_accessed=1, transcendentals=0)
VMEM_WHOLE = pl.BlockSpec(memory_space=pltpu.VMEM)
SMEM_WHOLE = pl.BlockSpec(memory_space=pltpu.SMEM)


def along_seq(value, dx, dy):
    pairs = [
        (x * SIDE + y, (x + dx) % SIDE * SIDE + (y + dy) % SIDE)
        for x in range(SIDE)
        for y in range(SIDE)
    ]
    return lax.ppermute(value, "seq", pairs)


def column(z, core):
    return (z % 2) * 4 + core * 2 + z // 2


def along_z(value, place):
    pairs = []
    for z in range(4):
        for core in range(2):
            pairs.append((column(z, core), column(*place(z, core))))
    return lax.ppermute(value, SECTION_HEAD, pairs)


def to_near(value):
    return along_z(value, lambda z, core: (z ^ 1, core))


def to_far(value):
    return along_z(value, lambda z, core: (3 - z, core))


def to_core(value):
    return along_z(value, lambda z, core: (z, 1 - core))


def project_body(selected_ref, x_ref, wk_ref, wv_ref, k_ref, v_ref, slots_ref, w_ref):
    step = pl.program_id(0)
    rows = x_ref.shape[0]
    steps = pl.num_programs(0)
    blocks_dev = (k_ref.shape[0] - NOTE_ROWS) // BLOCK
    blocks = SIDE * SIDE * blocks_dev

    @pl.when(step == 0)
    def _():
        w_ref[:, :HEAD_DIM] = wk_ref[...]
        w_ref[:, HEAD_DIM:] = wv_ref[...]
    @pl.when(step == steps - 1)
    def _():
        picked = selected_ref[...]
        tiles, per_tile = picked.shape
        source = lax.broadcasted_iota(jnp.int32, (per_tile, PICKS), 0)
        place = lax.broadcasted_iota(jnp.int32, (per_tile, PICKS), 1)
        repeat = (place % per_tile == source).astype(jnp.float32).astype(jnp.bfloat16)

        def repeated(part):
            part = part.astype(jnp.float32).astype(jnp.bfloat16)
            return jnp.dot(part, repeat, preferred_element_type=jnp.float32)

        wide = repeated(picked // blocks_dev) * blocks_dev + repeated(picked % blocks_dev)
        tile = lax.broadcasted_iota(jnp.int32, (tiles, PICKS), 0)
        at = lax.broadcasted_iota(jnp.int32, (tiles, PICKS), 1)
        ids = jnp.sum(jnp.where(at // per_tile == tile, wide, 0.0), axis=0, keepdims=True)

        block = lax.broadcasted_iota(jnp.int32, (blocks, PICKS), 0)
        hit = (block == ids.astype(jnp.int32)).astype(jnp.float32)
        wanted = jnp.broadcast_to(jnp.max(hit, axis=1, keepdims=True), (blocks, PICKS))
        one = lax.broadcasted_iota(jnp.int32, (blocks, blocks), 0)
        other = lax.broadcasted_iota(jnp.int32, (blocks, blocks), 1)
        before = (one // blocks_dev == other // blocks_dev) & (other < one)
        rank = jnp.dot(
            before.astype(jnp.float32).astype(jnp.bfloat16),
            wanted.astype(jnp.bfloat16),
            preferred_element_type=jnp.float32,
        )
        owner = block // blocks_dev
        slot = (owner * CAP).astype(jnp.float32) + rank
        slots = jnp.sum(hit * slot, axis=0, keepdims=True)
        slots_ref[...] = jnp.broadcast_to(slots, slots_ref.shape).astype(jnp.int32)
        place = lax.broadcasted_iota(jnp.int32, (blocks, PICKS), 1).astype(jnp.float32)
        local = (block % blocks_dev).astype(jnp.float32)
        asked = jnp.sum(
            jnp.where(slot == place, wanted * local, 0.0), axis=0, keepdims=True
        )
        note = jnp.broadcast_to(asked, (NOTE_ROWS, PICKS)).astype(jnp.bfloat16)
        k_ref[rows * steps :, :] = note
        v_ref[rows * steps :, :] = note

    both = jnp.dot(x_ref[...], w_ref[...], preferred_element_type=jnp.float32)
    at = pl.ds(pl.multiple_of(step * rows, rows), rows)
    k_ref[at, :] = both[:, :HEAD_DIM].astype(jnp.bfloat16)
    v_ref[at, :] = both[:, HEAD_DIM:].astype(jnp.bfloat16)


def in_hbm(value):
    return pltpu.with_memory_space_constraint(value, pltpu.HBM)


def project(image_features, key_weight, value_weight, selected):
    rows, enc = image_features.shape
    steps = 4
    out = jax.ShapeDtypeStruct((rows + NOTE_ROWS, HEAD_DIM), jnp.bfloat16)
    whole = lambda shape: pl.BlockSpec(shape, lambda i: (0,) * len(shape))
    return pl.pallas_call(
        project_body,
        grid=(steps,),
        in_specs=[
            whole(selected.shape),
            pl.BlockSpec((rows // steps, enc), lambda i: (i, 0)),
            whole((enc, HEAD_DIM)),
            whole((enc, HEAD_DIM)),
        ],
        out_specs=[
            whole((rows + NOTE_ROWS, HEAD_DIM)),
            whole((rows + NOTE_ROWS, HEAD_DIM)),
            whole((8, PICKS)),
        ],
        out_shape=[out, out, jax.ShapeDtypeStruct((8, PICKS), jnp.int32)],
        scratch_shapes=[pltpu.VMEM((enc, 2 * HEAD_DIM), jnp.bfloat16)],
        compiler_params=pltpu.CompilerParams(vmem_limit_bytes=40 << 20),
        cost_estimate=SMALL,
        name="project",
    )(selected, in_hbm(image_features), in_hbm(key_weight), in_hbm(value_weight))


def pack_one(ask, me, base, stride, ring, outs):
    for dest, out in enumerate(outs):
        for away, ref in enumerate(ring):
            first = base + ((me + away) & (SIDE - 1)) * stride
            for slot in range(CAP):
                block = pl.multiple_of(ask[dest, first + slot] * BLOCK, BLOCK)
                at = (away * CAP + slot) * BLOCK
                out[at : at + BLOCK, :] = ref[pl.ds(block, BLOCK), :]


def pack_body(place_ref, *refs):
    k_in, v_in, k_out, v_out = refs[:4], refs[4:8], refs[8:12], refs[12:16]
    note_ref, ask_ref, sem = refs[16:]

    def note(ring):
        last = lambda ref: ref[ref.shape[0] - NOTE_ROWS :, :].astype(jnp.float32)[:1]
        return jnp.concatenate([last(ref) for ref in ring], axis=0)

    notes = jnp.concatenate([note(v_in), note(k_in)], axis=0)
    note_ref[...] = notes.astype(jnp.int32)
    copy = pltpu.make_async_copy(note_ref, ask_ref, sem)
    copy.start()
    copy.wait()
    my_x, my_y = place_ref[0], place_ref[1]
    pack_one(ask_ref, my_x, my_y * CAP, SIDE * CAP, k_in, k_out)
    pack_one(ask_ref.at[SIDE:], my_y, my_x * (SIDE * CAP), CAP, v_in, v_out)


def pack(place, k_in, v_in):
    outs = [jax.ShapeDtypeStruct((SIDE * CAP * BLOCK, HEAD_DIM), jnp.bfloat16)] * SIDE
    out = pl.pallas_call(
        pack_body,
        in_specs=[SMEM_WHOLE] + [VMEM_WHOLE] * 8,
        out_specs=[VMEM_WHOLE] * 8,
        out_shape=outs + outs,
        scratch_shapes=[
            pltpu.VMEM((2 * SIDE, PICKS), jnp.int32),
            pltpu.SMEM((2 * SIDE, PICKS), jnp.int32),
            pltpu.SemaphoreType.DMA,
        ],
        compiler_params=pltpu.CompilerParams(vmem_limit_bytes=32 << 20),
        cost_estimate=SMALL,
        name="pack",
    )(place, *k_in, *v_in)
    return out[:4], out[4:]


def attend_body(first_tile, slots_ref, place_ref, q_ref, k_ref, v_ref, o_ref, kt, vt):
    my_x, my_y = place_ref[0], place_ref[1]
    for tile in range(o_ref.shape[0] // TILE):
        for pick in range(TOPK):
            slot = slots_ref[0, (first_tile + tile) * TOPK + pick]
            owner, rank = slot >> 3, slot & (CAP - 1)
            away_x = ((owner >> 2) - my_x) & (SIDE - 1)
            away_y = ((owner & 3) - my_y) & (SIDE - 1)
            k_at = (away_y * SIDE + away_x) * CAP + rank
            v_at = (away_x * SIDE + away_y) * CAP + rank
            to = slice(pick * BLOCK, (pick + 1) * BLOCK)
            kt[tile % 2, to, :] = k_ref[pl.ds(pl.multiple_of(k_at * BLOCK, BLOCK), BLOCK), :]
            vt[tile % 2, to, :] = v_ref[pl.ds(pl.multiple_of(v_at * BLOCK, BLOCK), BLOCK), :]
        rows = slice(tile * TILE, (tile + 1) * TILE)
        asking = slice((first_tile + tile) * TILE, (first_tile + tile + 1) * TILE)
        heads = [slice(h * HEAD_DIM, (h + 1) * HEAD_DIM) for h in range(GROUP)]
        stacked = jnp.concatenate([q_ref[asking, columns] for columns in heads], axis=0)
        scores = lax.dot_general(
            stacked, kt[tile % 2], (((1,), (1,)), ((), ())), preferred_element_type=jnp.float32
        )
        largest = jnp.max(scores, axis=-1, keepdims=True)
        exponent = jnp.exp2((scores - largest) * (SCALE * LOG2_E))
        total = jnp.sum(exponent, axis=-1, keepdims=True)
        weights = (exponent * (1.0 / total)).astype(jnp.bfloat16)
        mixed = jnp.dot(weights, vt[tile % 2], preferred_element_type=jnp.float32)
        mixed = mixed.astype(jnp.bfloat16)
        for h, columns in enumerate(heads):
            o_ref[rows, columns] = mixed[h * TILE : (h + 1) * TILE]


def attend(first_tile, tiles, slots, place, queries, keys, values):
    width = queries.shape[1]
    rows = tiles * TILE
    return pl.pallas_call(
        functools.partial(attend_body, first_tile),
        in_specs=[SMEM_WHOLE, SMEM_WHOLE] + [VMEM_WHOLE] * 3,
        out_specs=VMEM_WHOLE,
        out_shape=jax.ShapeDtypeStruct((rows, width), jnp.bfloat16),
        scratch_shapes=[pltpu.VMEM((2, TOPK * BLOCK, HEAD_DIM), jnp.bfloat16)] * 2,
        compiler_params=pltpu.CompilerParams(vmem_limit_bytes=32 << 20),
        cost_estimate=SMALL,
        name="attend",
    )(slots, place, queries, keys, values)


def pick_body(places_ref, w_ref, *out_refs):
    at = 0
    for ref in out_refs:
        ref[...] = w_ref[at : at + ref.shape[0], :]
        at += ref.shape[0]


def pick(places, weight, pieces):
    depth, width = weight.shape[0], weight.shape[1] // 8
    return pl.pallas_call(
        pick_body,
        grid_spec=pltpu.PrefetchScalarGridSpec(
            num_scalar_prefetch=1,
            grid=(4,),
            in_specs=[pl.BlockSpec((depth, width), lambda i, places: (0, places[i]))],
            out_specs=[pl.BlockSpec((rows, width), lambda i, places: (0, i)) for rows in pieces],
        ),
        out_shape=[jax.ShapeDtypeStruct((rows, 4 * width), weight.dtype) for rows in pieces],
        compiler_params=pltpu.CompilerParams(vmem_limit_bytes=8 << 20),
        cost_estimate=SMALL,
        name="pick",
    )(places, in_hbm(weight))


def multiply_body(mine_ref, near_ref, w_ref, *out_refs):
    left = jnp.concatenate([mine_ref[...], near_ref[...]], axis=1)
    width = w_ref.shape[1] // len(out_refs)
    for group, out_ref in enumerate(out_refs):
        columns = slice(group * width, (group + 1) * width)
        product = jnp.dot(left, w_ref[:, columns], preferred_element_type=jnp.float32)
        out_ref[...] = product.astype(out_ref.dtype)


def multiply(mine, near, weight):
    shape = (mine.shape[0], weight.shape[1] // 4)
    give = jax.ShapeDtypeStruct(shape, jnp.bfloat16)
    keep = jax.ShapeDtypeStruct(shape, jnp.float32)
    return pl.pallas_call(
        multiply_body,
        in_specs=[VMEM_WHOLE] * 3,
        out_specs=[VMEM_WHOLE] * 4,
        out_shape=[give, give, keep, keep],
        compiler_params=pltpu.CompilerParams(vmem_limit_bytes=24 << 20),
        cost_estimate=SMALL,
        name="multiply",
    )(mine, near, weight)


def rms_normed(text_hidden, norm_gain):
    as_float = text_hidden.astype(jnp.float32)
    inverse = lax.rsqrt(jnp.mean(as_float * as_float, axis=-1, keepdims=True) + EPSILON)
    return (as_float * inverse * norm_gain).astype(jnp.bfloat16)


def after(value, other):
    return lax.optimization_barrier((value, other))[0]


def spread(value, dx, dy, hold=lambda part: part):
    minus = along_seq(value, dx, dy)
    plus = along_seq(value, -dx, -dy)
    two = along_seq(hold(after(value, minus)), 2 * dx, 2 * dy)
    return value, plus, two, minus


def exchange(packed, dx, dy, hold=lambda part: part):
    here, up, across, down = packed
    minus = along_seq(up, dx, dy)
    plus = along_seq(down, -dx, -dy)
    two = along_seq(hold(after(across, minus)), 2 * dx, 2 * dy)
    return jnp.concatenate([here, plus, two, minus])


def shards(
    text_hidden,
    norm_gain,
    image_features,
    query_weight,
    key_weight,
    value_weight,
    output_weight,
    selected,
):
    seq = lax.axis_index("seq")
    my_x, my_y = seq // SIDE, seq % SIDE
    section, z_hi = lax.axis_index("section"), lax.axis_index("head")
    z, core = z_hi * 2 + section // 2, section % 2

    place = jnp.stack([my_x, my_y])

    def wanted_columns(z):
        return jnp.stack(
            [column(3 - z, 1 - core), column(z, 1 - core), column(3 - z, core), column(z, core)]
        )

    k_own, v_own, slots = project(image_features, key_weight, value_weight, selected)
    pieces = pick(wanted_columns(z ^ 1), after(output_weight, k_own), NEAR_PIECES)
    near_weight = []
    for piece in pieces:
        hold = near_weight[-1] if near_weight else text_hidden
        near_weight.append(to_near(after(piece, hold)))
    k_ring = spread(k_own, 1, 0)
    v_ring = spread(v_own, 0, 1)

    normed = rms_normed(after(text_hidden, k_own), norm_gain)
    queries = jnp.dot(normed, query_weight, preferred_element_type=jnp.float32).astype(jnp.bfloat16)

    k_out, v_out = pack(after(after(place, near_weight[0]), queries), k_ring, v_ring)
    keys = exchange(k_out, 0, 1)
    values = exchange(v_out, 1, 0, lambda part: after(part, near_weight[1]))
    own_weight = pick(
        wanted_columns(z), after(output_weight, k_out[0]), (output_weight.shape[0],)
    )
    weight = jnp.concatenate([*own_weight, *near_weight])

    starts = [sum(CHUNKS[:index]) for index in range(len(CHUNKS))]
    mine, near, sent, outs = [], [], [], []

    def attended(slots):
        index = len(mine)
        part = attend(starts[index], CHUNKS[index], slots, place, queries, keys, values)
        mine.append(part)
        near.append(to_near(part))
        return after(slots, part)

    while len(mine) < AHEAD:
        slots = attended(slots)
    weight = after(weight, mine[-1])
    last = len(CHUNKS) - 1
    for index in range(len(CHUNKS)):
        if index >= LAG:
            weight = after(weight, sent[index - LAG])
        if FIN and index >= FIN:
            weight = after(weight, outs[index - FIN])
        give_far, give_own, keep_far, keep_own = multiply(mine[index], near[index], weight)
        weight = after(weight, give_far)
        if len(mine) < len(CHUNKS):
            slots = attended(after(slots, give_far))
            weight = after(weight, mine[-1])
        got_far, got_own = to_core(give_far), to_core(give_own)
        if GOT and index >= GOT:
            got_far = after(got_far, outs[index - GOT])
        send = (keep_far + got_far.astype(jnp.float32)).astype(jnp.bfloat16)
        far = to_far(send)
        sent.append(send)
        total = keep_own + got_own.astype(jnp.float32) + far.astype(jnp.float32)
        outs.append(total.astype(jnp.bfloat16))
    return jnp.concatenate(outs, axis=0)


def solution(mesh):
    in_specs = (
        P("seq", None),
        P(),
        P("seq", None),
        P(None, ("section", "head")),
        P(None, ("section", "head")),
        P(None, ("section", "head")),
        P(("section", "head"), None),
        P("seq", None),
    )
    out_specs = P("seq", ("section", "head"))
    return jax.shard_map(shards, mesh=mesh, in_specs=in_specs, out_specs=out_specs, check_vma=False)
```

```python
import functools

import jax
import jax.numpy as jnp
from jax import lax
from jax.experimental import pallas as pl
from jax.experimental.pallas import tpu as pltpu
from jax.sharding import PartitionSpec as P

HEADS = 32
KV_HEADS = 8
HEAD_DIM = 128
GROUP = HEADS // KV_HEADS
TILE = 128
BLOCK = 64
TOPK = 16
SIDE = 4
CAP = 8
PICKS = SIDE * SIDE * CAP
NOTE_ROWS = 16
EPSILON = 1e-05
NEAR_PIECES = (64, 160, 160, 128)
CHUNKS = (2, 2, 2, 2)
AHEAD = 3
LAG = 2
SCALE = HEAD_DIM**-0.5
LOG2_E = 1.4426950408889634

SECTION_HEAD = ("section", "head")
SMALL = pl.CostEstimate(flops=1, bytes_accessed=1, transcendentals=0)
VMEM_WHOLE = pl.BlockSpec(memory_space=pltpu.VMEM)
SMEM_WHOLE = pl.BlockSpec(memory_space=pltpu.SMEM)


def along_seq(value, dx, dy):
    pairs = [
        (x * SIDE + y, (x + dx) % SIDE * SIDE + (y + dy) % SIDE)
        for x in range(SIDE)
        for y in range(SIDE)
    ]
    return lax.ppermute(value, "seq", pairs)


def column(z, core):
    return (z % 2) * 4 + core * 2 + z // 2


def along_z(value, place):
    pairs = []
    for z in range(4):
        for core in range(2):
            pairs.append((column(z, core), column(*place(z, core))))
    return lax.ppermute(value, SECTION_HEAD, pairs)


def to_near(value):
    return along_z(value, lambda z, core: (z ^ 1, core))


def to_far(value):
    return along_z(value, lambda z, core: (3 - z, core))


def to_core(value):
    return along_z(value, lambda z, core: (z, 1 - core))


def project_body(selected_ref, x_ref, wk_ref, wv_ref, k_ref, v_ref, slots_ref, w_ref):
    step = pl.program_id(0)
    rows = x_ref.shape[0]
    steps = pl.num_programs(0)
    blocks_dev = (k_ref.shape[0] - NOTE_ROWS) // BLOCK
    blocks = SIDE * SIDE * blocks_dev

    @pl.when(step == 0)
    def _():
        w_ref[:, :HEAD_DIM] = wk_ref[...]
        w_ref[:, HEAD_DIM:] = wv_ref[...]
    @pl.when(step == steps - 1)
    def _():
        picked = selected_ref[...]
        tiles, per_tile = picked.shape
        source = lax.broadcasted_iota(jnp.int32, (per_tile, PICKS), 0)
        place = lax.broadcasted_iota(jnp.int32, (per_tile, PICKS), 1)
        repeat = (place % per_tile == source).astype(jnp.float32).astype(jnp.bfloat16)

        def repeated(part):
            part = part.astype(jnp.float32).astype(jnp.bfloat16)
            return jnp.dot(part, repeat, preferred_element_type=jnp.float32)

        wide = repeated(picked // blocks_dev) * blocks_dev + repeated(picked % blocks_dev)
        tile = lax.broadcasted_iota(jnp.int32, (tiles, PICKS), 0)
        at = lax.broadcasted_iota(jnp.int32, (tiles, PICKS), 1)
        ids = jnp.sum(jnp.where(at // per_tile == tile, wide, 0.0), axis=0, keepdims=True)

        block = lax.broadcasted_iota(jnp.int32, (blocks, PICKS), 0)
        hit = (block == ids.astype(jnp.int32)).astype(jnp.float32)
        wanted = jnp.broadcast_to(jnp.max(hit, axis=1, keepdims=True), (blocks, PICKS))
        one = lax.broadcasted_iota(jnp.int32, (blocks, blocks), 0)
        other = lax.broadcasted_iota(jnp.int32, (blocks, blocks), 1)
        before = (one // blocks_dev == other // blocks_dev) & (other < one)
        rank = jnp.dot(
            before.astype(jnp.float32).astype(jnp.bfloat16),
            wanted.astype(jnp.bfloat16),
            preferred_element_type=jnp.float32,
        )
        owner = block // blocks_dev
        slot = (owner * CAP).astype(jnp.float32) + rank
        slots = jnp.sum(hit * slot, axis=0, keepdims=True)
        slots_ref[...] = jnp.broadcast_to(slots, slots_ref.shape).astype(jnp.int32)
        place = lax.broadcasted_iota(jnp.int32, (blocks, PICKS), 1).astype(jnp.float32)
        local = (block % blocks_dev).astype(jnp.float32)
        asked = jnp.sum(
            jnp.where(slot == place, wanted * local, 0.0), axis=0, keepdims=True
        )
        note = jnp.broadcast_to(asked, (NOTE_ROWS, PICKS)).astype(jnp.bfloat16)
        k_ref[rows * steps :, :] = note
        v_ref[rows * steps :, :] = note

    both = jnp.dot(x_ref[...], w_ref[...], preferred_element_type=jnp.float32)
    at = pl.ds(pl.multiple_of(step * rows, rows), rows)
    k_ref[at, :] = both[:, :HEAD_DIM].astype(jnp.bfloat16)
    v_ref[at, :] = both[:, HEAD_DIM:].astype(jnp.bfloat16)


def in_hbm(value):
    return pltpu.with_memory_space_constraint(value, pltpu.HBM)


def project(image_features, key_weight, value_weight, selected):
    rows, enc = image_features.shape
    steps = 4
    out = jax.ShapeDtypeStruct((rows + NOTE_ROWS, HEAD_DIM), jnp.bfloat16)
    whole = lambda shape: pl.BlockSpec(shape, lambda i: (0,) * len(shape))
    return pl.pallas_call(
        project_body,
        grid=(steps,),
        in_specs=[
            whole(selected.shape),
            pl.BlockSpec((rows // steps, enc), lambda i: (i, 0)),
            whole((enc, HEAD_DIM)),
            whole((enc, HEAD_DIM)),
        ],
        out_specs=[
            whole((rows + NOTE_ROWS, HEAD_DIM)),
            whole((rows + NOTE_ROWS, HEAD_DIM)),
            whole((8, PICKS)),
        ],
        out_shape=[out, out, jax.ShapeDtypeStruct((8, PICKS), jnp.int32)],
        scratch_shapes=[pltpu.VMEM((enc, 2 * HEAD_DIM), jnp.bfloat16)],
        compiler_params=pltpu.CompilerParams(vmem_limit_bytes=40 << 20),
        cost_estimate=SMALL,
        name="project",
    )(selected, in_hbm(image_features), in_hbm(key_weight), in_hbm(value_weight))


def pack_one(ask, me, base, stride, ring, outs):
    for dest, out in enumerate(outs):
        for away, ref in enumerate(ring):
            first = base + ((me + away) & (SIDE - 1)) * stride
            for slot in range(CAP):
                block = pl.multiple_of(ask[dest, first + slot] * BLOCK, BLOCK)
                at = (away * CAP + slot) * BLOCK
                out[at : at + BLOCK, :] = ref[pl.ds(block, BLOCK), :]


def pack_body(place_ref, *refs):
    k_in, v_in, k_out, v_out = refs[:4], refs[4:8], refs[8:12], refs[12:16]
    note_ref, ask_ref, sem = refs[16:]

    def note(ring):
        last = lambda ref: ref[ref.shape[0] - NOTE_ROWS :, :].astype(jnp.float32)[:1]
        return jnp.concatenate([last(ref) for ref in ring], axis=0)

    notes = jnp.concatenate([note(v_in), note(k_in)], axis=0)
    note_ref[...] = notes.astype(jnp.int32)
    copy = pltpu.make_async_copy(note_ref, ask_ref, sem)
    copy.start()
    copy.wait()
    my_x, my_y = place_ref[0], place_ref[1]
    pack_one(ask_ref, my_x, my_y * CAP, SIDE * CAP, k_in, k_out)
    pack_one(ask_ref.at[SIDE:], my_y, my_x * (SIDE * CAP), CAP, v_in, v_out)


def pack(place, k_in, v_in):
    outs = [jax.ShapeDtypeStruct((SIDE * CAP * BLOCK, HEAD_DIM), jnp.bfloat16)] * SIDE
    out = pl.pallas_call(
        pack_body,
        in_specs=[SMEM_WHOLE] + [VMEM_WHOLE] * 8,
        out_specs=[VMEM_WHOLE] * 8,
        out_shape=outs + outs,
        scratch_shapes=[
            pltpu.VMEM((2 * SIDE, PICKS), jnp.int32),
            pltpu.SMEM((2 * SIDE, PICKS), jnp.int32),
            pltpu.SemaphoreType.DMA,
        ],
        compiler_params=pltpu.CompilerParams(vmem_limit_bytes=32 << 20),
        cost_estimate=SMALL,
        name="pack",
    )(place, *k_in, *v_in)
    return out[:4], out[4:]


def attend_body(first_tile, slots_ref, place_ref, q_ref, k_ref, v_ref, o_ref, kt, vt):
    my_x, my_y = place_ref[0], place_ref[1]
    for tile in range(o_ref.shape[0] // TILE):
        for pick in range(TOPK):
            slot = slots_ref[0, (first_tile + tile) * TOPK + pick]
            owner, rank = slot >> 3, slot & (CAP - 1)
            away_x = ((owner >> 2) - my_x) & (SIDE - 1)
            away_y = ((owner & 3) - my_y) & (SIDE - 1)
            k_at = (away_y * SIDE + away_x) * CAP + rank
            v_at = (away_x * SIDE + away_y) * CAP + rank
            to = slice(pick * BLOCK, (pick + 1) * BLOCK)
            kt[tile % 2, to, :] = k_ref[pl.ds(pl.multiple_of(k_at * BLOCK, BLOCK), BLOCK), :]
            vt[tile % 2, to, :] = v_ref[pl.ds(pl.multiple_of(v_at * BLOCK, BLOCK), BLOCK), :]
        rows = slice(tile * TILE, (tile + 1) * TILE)
        asking = slice((first_tile + tile) * TILE, (first_tile + tile + 1) * TILE)
        heads = [slice(h * HEAD_DIM, (h + 1) * HEAD_DIM) for h in range(GROUP)]
        stacked = jnp.concatenate([q_ref[asking, columns] for columns in heads], axis=0)
        scores = lax.dot_general(
            stacked, kt[tile % 2], (((1,), (1,)), ((), ())), preferred_element_type=jnp.float32
        )
        largest = jnp.max(scores, axis=-1, keepdims=True)
        exponent = jnp.exp2((scores - largest) * (SCALE * LOG2_E))
        total = jnp.sum(exponent, axis=-1, keepdims=True)
        weights = (exponent * (1.0 / total)).astype(jnp.bfloat16)
        mixed = jnp.dot(weights, vt[tile % 2], preferred_element_type=jnp.float32)
        mixed = mixed.astype(jnp.bfloat16)
        for h, columns in enumerate(heads):
            o_ref[rows, columns] = mixed[h * TILE : (h + 1) * TILE]


def attend(first_tile, tiles, slots, place, queries, keys, values):
    width = queries.shape[1]
    rows = tiles * TILE
    return pl.pallas_call(
        functools.partial(attend_body, first_tile),
        in_specs=[SMEM_WHOLE, SMEM_WHOLE] + [VMEM_WHOLE] * 3,
        out_specs=VMEM_WHOLE,
        out_shape=jax.ShapeDtypeStruct((rows, width), jnp.bfloat16),
        scratch_shapes=[pltpu.VMEM((2, TOPK * BLOCK, HEAD_DIM), jnp.bfloat16)] * 2,
        compiler_params=pltpu.CompilerParams(vmem_limit_bytes=32 << 20),
        cost_estimate=SMALL,
        name="attend",
    )(slots, place, queries, keys, values)


def pick_body(places_ref, w_ref, *out_refs):
    at = 0
    for ref in out_refs:
        ref[...] = w_ref[at : at + ref.shape[0], :]
        at += ref.shape[0]


def pick(places, weight, pieces):
    depth, width = weight.shape[0], weight.shape[1] // 8
    return pl.pallas_call(
        pick_body,
        grid_spec=pltpu.PrefetchScalarGridSpec(
            num_scalar_prefetch=1,
            grid=(4,),
            in_specs=[pl.BlockSpec((depth, width), lambda i, places: (0, places[i]))],
            out_specs=[pl.BlockSpec((rows, width), lambda i, places: (0, i)) for rows in pieces],
        ),
        out_shape=[jax.ShapeDtypeStruct((rows, 4 * width), weight.dtype) for rows in pieces],
        compiler_params=pltpu.CompilerParams(vmem_limit_bytes=8 << 20),
        cost_estimate=SMALL,
        name="pick",
    )(places, in_hbm(weight))


def multiply_body(mine_ref, near_ref, w_ref, *out_refs):
    left = jnp.concatenate([mine_ref[...], near_ref[...]], axis=1)
    width = w_ref.shape[1] // len(out_refs)
    for group, out_ref in enumerate(out_refs):
        columns = slice(group * width, (group + 1) * width)
        product = jnp.dot(left, w_ref[:, columns], preferred_element_type=jnp.float32)
        out_ref[...] = product.astype(out_ref.dtype)


def multiply(mine, near, weight):
    shape = (mine.shape[0], weight.shape[1] // 4)
    give = jax.ShapeDtypeStruct(shape, jnp.bfloat16)
    keep = jax.ShapeDtypeStruct(shape, jnp.float32)
    return pl.pallas_call(
        multiply_body,
        in_specs=[VMEM_WHOLE] * 3,
        out_specs=[VMEM_WHOLE] * 4,
        out_shape=[give, give, keep, keep],
        compiler_params=pltpu.CompilerParams(vmem_limit_bytes=24 << 20),
        cost_estimate=SMALL,
        name="multiply",
    )(mine, near, weight)


def ask_body(x_ref, gain_ref, w_ref, o_ref):
    as_float = x_ref[...].astype(jnp.float32)
    mean = jnp.mean(as_float * as_float, axis=-1, keepdims=True)
    normed = (as_float * lax.rsqrt(mean + EPSILON) * gain_ref[...]).astype(jnp.bfloat16)
    product = jnp.dot(normed, w_ref[...], preferred_element_type=jnp.float32)
    o_ref[...] = product.astype(jnp.bfloat16)


def queries_of(text_hidden, norm_gain, query_weight):
    (rows, depth), width = text_hidden.shape, query_weight.shape[1]
    steps = 4
    return pl.pallas_call(
        ask_body,
        grid=(steps,),
        in_specs=[
            pl.BlockSpec((rows // steps, depth), lambda i: (i, 0)),
            pl.BlockSpec((1, depth), lambda i: (0, 0)),
            pl.BlockSpec((depth, width), lambda i: (0, 0)),
        ],
        out_specs=pl.BlockSpec((rows // steps, width), lambda i: (i, 0)),
        out_shape=jax.ShapeDtypeStruct((rows, width), jnp.bfloat16),
        compiler_params=pltpu.CompilerParams(vmem_limit_bytes=32 << 20),
        cost_estimate=SMALL,
        name="ask",
    )(in_hbm(text_hidden), norm_gain.reshape(1, depth), in_hbm(query_weight))


def after(value, other):
    return lax.optimization_barrier((value, other))[0]


def spread(value, dx, dy, hold=lambda part: part):
    minus = along_seq(value, dx, dy)
    plus = along_seq(value, -dx, -dy)
    two = along_seq(hold(after(value, minus)), 2 * dx, 2 * dy)
    return value, plus, two, minus


def exchange(packed, dx, dy, hold=lambda part: part):
    here, up, across, down = packed
    minus = along_seq(up, dx, dy)
    plus = along_seq(down, -dx, -dy)
    two = along_seq(hold(after(across, minus)), 2 * dx, 2 * dy)
    return jnp.concatenate([here, plus, two, minus])


def shards(
    text_hidden,
    norm_gain,
    image_features,
    query_weight,
    key_weight,
    value_weight,
    output_weight,
    selected,
):
    seq = lax.axis_index("seq")
    my_x, my_y = seq // SIDE, seq % SIDE
    section, z_hi = lax.axis_index("section"), lax.axis_index("head")
    z, core = z_hi * 2 + section // 2, section % 2

    place = jnp.stack([my_x, my_y])

    def wanted_columns(z):
        return jnp.stack(
            [column(3 - z, 1 - core), column(z, 1 - core), column(3 - z, core), column(z, core)]
        )

    k_own, v_own, slots = project(image_features, key_weight, value_weight, selected)
    pieces = pick(wanted_columns(z ^ 1), after(output_weight, k_own), NEAR_PIECES)
    k_ring = spread(k_own, 1, 0, lambda part: after(part, pieces[0]))
    v_ring = spread(v_own, 0, 1)
    near_weight = []
    for piece in pieces:
        near_weight.append(to_near(after(piece, near_weight[-1] if near_weight else k_ring[3])))

    queries = queries_of(after(text_hidden, k_own), norm_gain, query_weight)

    k_out, v_out = pack(after(after(place, near_weight[0]), queries), k_ring, v_ring)
    keys = exchange(k_out, 0, 1)
    values = exchange(v_out, 1, 0, lambda part: after(part, near_weight[1]))
    own_weight = pick(
        wanted_columns(z), after(output_weight, k_out[0]), (output_weight.shape[0],)
    )
    weight = jnp.concatenate([*own_weight, *near_weight])

    starts = [sum(CHUNKS[:index]) for index in range(len(CHUNKS))]
    mine, near, sent, outs = [], [], [], []

    def attended(slots):
        index = len(mine)
        part = attend(starts[index], CHUNKS[index], slots, place, queries, keys, values)
        mine.append(part)
        near.append(to_near(part))
        return after(slots, part)

    while len(mine) < AHEAD:
        slots = attended(slots)
    weight = after(weight, mine[-1])
    last = len(CHUNKS) - 1
    for index in range(len(CHUNKS)):
        if index >= LAG:
            weight = after(weight, sent[index - LAG])
        if index >= 3:
            weight = after(weight, outs[index - 3])
        give_far, give_own, keep_far, keep_own = multiply(mine[index], near[index], weight)
        weight = after(weight, give_far)
        if len(mine) < len(CHUNKS):
            slots = attended(after(slots, give_far))
            weight = after(weight, mine[-1])
        got_far, got_own = to_core(give_far), to_core(give_own)
        if index >= 2 and index == last:
            got_far = after(got_far, outs[index - 2])
        send = (keep_far + got_far.astype(jnp.float32)).astype(jnp.bfloat16)
        far = to_far(send)
        sent.append(send)
        total = keep_own + got_own.astype(jnp.float32) + far.astype(jnp.float32)
        outs.append(total.astype(jnp.bfloat16))
    return jnp.concatenate(outs, axis=0)


def solution(mesh):
    in_specs = (
        P("seq", None),
        P(),
        P("seq", None),
        P(None, ("section", "head")),
        P(None, ("section", "head")),
        P(None, ("section", "head")),
        P(("section", "head"), None),
        P("seq", None),
    )
    out_specs = P("seq", ("section", "head"))
    return jax.shard_map(shards, mesh=mesh, in_specs=in_specs, out_specs=out_specs, check_vma=False)
```

```python
import functools

import jax
import jax.numpy as jnp
from jax import lax
from jax.experimental import pallas as pl
from jax.experimental.pallas import tpu as pltpu
from jax.sharding import PartitionSpec as P

HEADS = 32
KV_HEADS = 8
HEAD_DIM = 128
GROUP = HEADS // KV_HEADS
TILE = 128
BLOCK = 64
TOPK = 16
SIDE = 4
CAP = 8
PICKS = SIDE * SIDE * CAP
NOTE_ROWS = 16
EPSILON = 1e-05
NEAR_PIECES = (112, 144, 128, 128)
CHUNKS = (2, 2, 2, 2)
AHEAD = 3
LAG = 2
SCALE = HEAD_DIM**-0.5
LOG2_E = 1.4426950408889634

SECTION_HEAD = ("section", "head")
SMALL = pl.CostEstimate(flops=1, bytes_accessed=1, transcendentals=0)
VMEM_WHOLE = pl.BlockSpec(memory_space=pltpu.VMEM)
SMEM_WHOLE = pl.BlockSpec(memory_space=pltpu.SMEM)


def along_seq(value, dx, dy):
    pairs = [
        (x * SIDE + y, (x + dx) % SIDE * SIDE + (y + dy) % SIDE)
        for x in range(SIDE)
        for y in range(SIDE)
    ]
    return lax.ppermute(value, "seq", pairs)


def column(z, core):
    return (z % 2) * 4 + core * 2 + z // 2


def along_z(value, place):
    pairs = []
    for z in range(4):
        for core in range(2):
            pairs.append((column(z, core), column(*place(z, core))))
    return lax.ppermute(value, SECTION_HEAD, pairs)


def to_near(value):
    return along_z(value, lambda z, core: (z ^ 1, core))


def to_far(value):
    return along_z(value, lambda z, core: (3 - z, core))


def to_core(value):
    return along_z(value, lambda z, core: (z, 1 - core))


def project_body(selected_ref, x_ref, wk_ref, wv_ref, k_ref, v_ref, slots_ref, w_ref):
    step = pl.program_id(0)
    rows = x_ref.shape[0]
    steps = pl.num_programs(0)
    blocks_dev = (k_ref.shape[0] - NOTE_ROWS) // BLOCK
    blocks = SIDE * SIDE * blocks_dev

    @pl.when(step == 0)
    def _():
        w_ref[:, :HEAD_DIM] = wk_ref[...]
        w_ref[:, HEAD_DIM:] = wv_ref[...]
    @pl.when(step == steps - 1)
    def _():
        picked = selected_ref[...]
        tiles, per_tile = picked.shape
        source = lax.broadcasted_iota(jnp.int32, (per_tile, PICKS), 0)
        place = lax.broadcasted_iota(jnp.int32, (per_tile, PICKS), 1)
        repeat = (place % per_tile == source).astype(jnp.float32).astype(jnp.bfloat16)

        def repeated(part):
            part = part.astype(jnp.float32).astype(jnp.bfloat16)
            return jnp.dot(part, repeat, preferred_element_type=jnp.float32)

        wide = repeated(picked // blocks_dev) * blocks_dev + repeated(picked % blocks_dev)
        tile = lax.broadcasted_iota(jnp.int32, (tiles, PICKS), 0)
        at = lax.broadcasted_iota(jnp.int32, (tiles, PICKS), 1)
        ids = jnp.sum(jnp.where(at // per_tile == tile, wide, 0.0), axis=0, keepdims=True)

        block = lax.broadcasted_iota(jnp.int32, (blocks, PICKS), 0)
        hit = (block == ids.astype(jnp.int32)).astype(jnp.float32)
        wanted = jnp.broadcast_to(jnp.max(hit, axis=1, keepdims=True), (blocks, PICKS))
        one = lax.broadcasted_iota(jnp.int32, (blocks, blocks), 0)
        other = lax.broadcasted_iota(jnp.int32, (blocks, blocks), 1)
        before = (one // blocks_dev == other // blocks_dev) & (other < one)
        rank = jnp.dot(
            before.astype(jnp.float32).astype(jnp.bfloat16),
            wanted.astype(jnp.bfloat16),
            preferred_element_type=jnp.float32,
        )
        owner = block // blocks_dev
        slot = (owner * CAP).astype(jnp.float32) + rank
        slots = jnp.sum(hit * slot, axis=0, keepdims=True)
        slots_ref[...] = jnp.broadcast_to(slots, slots_ref.shape).astype(jnp.int32)
        place = lax.broadcasted_iota(jnp.int32, (blocks, PICKS), 1).astype(jnp.float32)
        local = (block % blocks_dev).astype(jnp.float32)
        asked = jnp.sum(
            jnp.where(slot == place, wanted * local, 0.0), axis=0, keepdims=True
        )
        note = jnp.broadcast_to(asked, (NOTE_ROWS, PICKS)).astype(jnp.bfloat16)
        k_ref[rows * steps :, :] = note
        v_ref[rows * steps :, :] = note

    both = jnp.dot(x_ref[...], w_ref[...], preferred_element_type=jnp.float32)
    at = pl.ds(pl.multiple_of(step * rows, rows), rows)
    k_ref[at, :] = both[:, :HEAD_DIM].astype(jnp.bfloat16)
    v_ref[at, :] = both[:, HEAD_DIM:].astype(jnp.bfloat16)


def in_hbm(value):
    return pltpu.with_memory_space_constraint(value, pltpu.HBM)


def project(image_features, key_weight, value_weight, selected):
    rows, enc = image_features.shape
    steps = 4
    out = jax.ShapeDtypeStruct((rows + NOTE_ROWS, HEAD_DIM), jnp.bfloat16)
    whole = lambda shape: pl.BlockSpec(shape, lambda i: (0,) * len(shape))
    return pl.pallas_call(
        project_body,
        grid=(steps,),
        in_specs=[
            whole(selected.shape),
            pl.BlockSpec((rows // steps, enc), lambda i: (i, 0)),
            whole((enc, HEAD_DIM)),
            whole((enc, HEAD_DIM)),
        ],
        out_specs=[
            whole((rows + NOTE_ROWS, HEAD_DIM)),
            whole((rows + NOTE_ROWS, HEAD_DIM)),
            whole((8, PICKS)),
        ],
        out_shape=[out, out, jax.ShapeDtypeStruct((8, PICKS), jnp.int32)],
        scratch_shapes=[pltpu.VMEM((enc, 2 * HEAD_DIM), jnp.bfloat16)],
        compiler_params=pltpu.CompilerParams(vmem_limit_bytes=40 << 20),
        cost_estimate=SMALL,
        name="project",
    )(selected, in_hbm(image_features), in_hbm(key_weight), in_hbm(value_weight))


def pack_one(ask, me, base, stride, ring, outs):
    for dest, out in enumerate(outs):
        for away, ref in enumerate(ring):
            first = base + ((me + away) & (SIDE - 1)) * stride
            for slot in range(CAP):
                block = pl.multiple_of(ask[dest, first + slot] * BLOCK, BLOCK)
                at = (away * CAP + slot) * BLOCK
                out[at : at + BLOCK, :] = ref[pl.ds(block, BLOCK), :]


def pack_body(place_ref, *refs):
    k_in, v_in, k_out, v_out = refs[:4], refs[4:8], refs[8:12], refs[12:16]
    note_ref, ask_ref, sem = refs[16:]

    def note(ring):
        last = lambda ref: ref[ref.shape[0] - NOTE_ROWS :, :].astype(jnp.float32)[:1]
        return jnp.concatenate([last(ref) for ref in ring], axis=0)

    notes = jnp.concatenate([note(v_in), note(k_in)], axis=0)
    note_ref[...] = notes.astype(jnp.int32)
    copy = pltpu.make_async_copy(note_ref, ask_ref, sem)
    copy.start()
    copy.wait()
    my_x, my_y = place_ref[0], place_ref[1]
    pack_one(ask_ref, my_x, my_y * CAP, SIDE * CAP, k_in, k_out)
    pack_one(ask_ref.at[SIDE:], my_y, my_x * (SIDE * CAP), CAP, v_in, v_out)


def pack(place, k_in, v_in):
    outs = [jax.ShapeDtypeStruct((SIDE * CAP * BLOCK, HEAD_DIM), jnp.bfloat16)] * SIDE
    out = pl.pallas_call(
        pack_body,
        in_specs=[SMEM_WHOLE] + [VMEM_WHOLE] * 8,
        out_specs=[VMEM_WHOLE] * 8,
        out_shape=outs + outs,
        scratch_shapes=[
            pltpu.VMEM((2 * SIDE, PICKS), jnp.int32),
            pltpu.SMEM((2 * SIDE, PICKS), jnp.int32),
            pltpu.SemaphoreType.DMA,
        ],
        compiler_params=pltpu.CompilerParams(vmem_limit_bytes=32 << 20),
        cost_estimate=SMALL,
        name="pack",
    )(place, *k_in, *v_in)
    return out[:4], out[4:]


def attend_body(first_tile, slots_ref, place_ref, q_ref, k_ref, v_ref, o_ref, kt, vt):
    my_x, my_y = place_ref[0], place_ref[1]
    for tile in range(o_ref.shape[0] // TILE):
        for pick in range(TOPK):
            slot = slots_ref[0, (first_tile + tile) * TOPK + pick]
            owner, rank = slot >> 3, slot & (CAP - 1)
            away_x = ((owner >> 2) - my_x) & (SIDE - 1)
            away_y = ((owner & 3) - my_y) & (SIDE - 1)
            k_at = (away_y * SIDE + away_x) * CAP + rank
            v_at = (away_x * SIDE + away_y) * CAP + rank
            to = slice(pick * BLOCK, (pick + 1) * BLOCK)
            kt[tile % 2, to, :] = k_ref[pl.ds(pl.multiple_of(k_at * BLOCK, BLOCK), BLOCK), :]
            vt[tile % 2, to, :] = v_ref[pl.ds(pl.multiple_of(v_at * BLOCK, BLOCK), BLOCK), :]
        rows = slice(tile * TILE, (tile + 1) * TILE)
        asking = slice((first_tile + tile) * TILE, (first_tile + tile + 1) * TILE)
        heads = [slice(h * HEAD_DIM, (h + 1) * HEAD_DIM) for h in range(GROUP)]
        stacked = jnp.concatenate([q_ref[asking, columns] for columns in heads], axis=0)
        scores = lax.dot_general(
            stacked, kt[tile % 2], (((1,), (1,)), ((), ())), preferred_element_type=jnp.float32
        )
        largest = jnp.max(scores, axis=-1, keepdims=True)
        exponent = jnp.exp2((scores - largest) * (SCALE * LOG2_E))
        total = jnp.sum(exponent, axis=-1, keepdims=True)
        weights = (exponent * (1.0 / total)).astype(jnp.bfloat16)
        mixed = jnp.dot(weights, vt[tile % 2], preferred_element_type=jnp.float32)
        mixed = mixed.astype(jnp.bfloat16)
        for h, columns in enumerate(heads):
            o_ref[rows, columns] = mixed[h * TILE : (h + 1) * TILE]


def attend(first_tile, tiles, slots, place, queries, keys, values):
    width = queries.shape[1]
    rows = tiles * TILE
    return pl.pallas_call(
        functools.partial(attend_body, first_tile),
        in_specs=[SMEM_WHOLE, SMEM_WHOLE] + [VMEM_WHOLE] * 3,
        out_specs=VMEM_WHOLE,
        out_shape=jax.ShapeDtypeStruct((rows, width), jnp.bfloat16),
        scratch_shapes=[pltpu.VMEM((2, TOPK * BLOCK, HEAD_DIM), jnp.bfloat16)] * 2,
        compiler_params=pltpu.CompilerParams(vmem_limit_bytes=32 << 20),
        cost_estimate=SMALL,
        name="attend",
    )(slots, place, queries, keys, values)


def pick_body(places_ref, w_ref, *out_refs):
    at = 0
    for ref in out_refs:
        ref[...] = w_ref[at : at + ref.shape[0], :]
        at += ref.shape[0]


def pick(places, weight, pieces):
    depth, width = weight.shape[0], weight.shape[1] // 8
    return pl.pallas_call(
        pick_body,
        grid_spec=pltpu.PrefetchScalarGridSpec(
            num_scalar_prefetch=1,
            grid=(4,),
            in_specs=[pl.BlockSpec((depth, width), lambda i, places: (0, places[i]))],
            out_specs=[pl.BlockSpec((rows, width), lambda i, places: (0, i)) for rows in pieces],
        ),
        out_shape=[jax.ShapeDtypeStruct((rows, 4 * width), weight.dtype) for rows in pieces],
        compiler_params=pltpu.CompilerParams(vmem_limit_bytes=8 << 20),
        cost_estimate=SMALL,
        name="pick",
    )(places, in_hbm(weight))


def multiply_body(mine_ref, near_ref, w_ref, *out_refs):
    left = jnp.concatenate([mine_ref[...], near_ref[...]], axis=1)
    width = w_ref.shape[1] // len(out_refs)
    for group, out_ref in enumerate(out_refs):
        columns = slice(group * width, (group + 1) * width)
        product = jnp.dot(left, w_ref[:, columns], preferred_element_type=jnp.float32)
        out_ref[...] = product.astype(out_ref.dtype)


def multiply(mine, near, weight):
    shape = (mine.shape[0], weight.shape[1] // 4)
    give = jax.ShapeDtypeStruct(shape, jnp.bfloat16)
    keep = jax.ShapeDtypeStruct(shape, jnp.float32)
    return pl.pallas_call(
        multiply_body,
        in_specs=[VMEM_WHOLE] * 3,
        out_specs=[VMEM_WHOLE] * 4,
        out_shape=[give, give, keep, keep],
        compiler_params=pltpu.CompilerParams(vmem_limit_bytes=24 << 20),
        cost_estimate=SMALL,
        name="multiply",
    )(mine, near, weight)


def ask_body(x_ref, gain_ref, w_ref, o_ref):
    as_float = x_ref[...].astype(jnp.float32)
    mean = jnp.mean(as_float * as_float, axis=-1, keepdims=True)
    normed = (as_float * lax.rsqrt(mean + EPSILON) * gain_ref[...]).astype(jnp.bfloat16)
    product = jnp.dot(normed, w_ref[...], preferred_element_type=jnp.float32)
    o_ref[...] = product.astype(jnp.bfloat16)


def queries_of(text_hidden, norm_gain, query_weight):
    (rows, depth), width = text_hidden.shape, query_weight.shape[1]
    steps = 4
    return pl.pallas_call(
        ask_body,
        grid=(steps,),
        in_specs=[
            pl.BlockSpec((rows // steps, depth), lambda i: (i, 0)),
            pl.BlockSpec((1, depth), lambda i: (0, 0)),
            pl.BlockSpec((depth, width), lambda i: (0, 0)),
        ],
        out_specs=pl.BlockSpec((rows // steps, width), lambda i: (i, 0)),
        out_shape=jax.ShapeDtypeStruct((rows, width), jnp.bfloat16),
        compiler_params=pltpu.CompilerParams(vmem_limit_bytes=32 << 20),
        cost_estimate=SMALL,
        name="ask",
    )(in_hbm(text_hidden), norm_gain.reshape(1, depth), in_hbm(query_weight))


def after(value, other):
    return lax.optimization_barrier((value, other))[0]


def spread(value, dx, dy, hold=lambda part: part):
    minus = along_seq(value, dx, dy)
    plus = along_seq(value, -dx, -dy)
    two = along_seq(hold(after(value, minus)), 2 * dx, 2 * dy)
    return value, plus, two, minus


def exchange(packed, dx, dy, hold=lambda part: part):
    here, up, across, down = packed
    minus = along_seq(up, dx, dy)
    plus = along_seq(down, -dx, -dy)
    two = along_seq(hold(after(across, minus)), 2 * dx, 2 * dy)
    return jnp.concatenate([here, plus, two, minus])


def shards(
    text_hidden,
    norm_gain,
    image_features,
    query_weight,
    key_weight,
    value_weight,
    output_weight,
    selected,
):
    seq = lax.axis_index("seq")
    my_x, my_y = seq // SIDE, seq % SIDE
    section, z_hi = lax.axis_index("section"), lax.axis_index("head")
    z, core = z_hi * 2 + section // 2, section % 2

    place = jnp.stack([my_x, my_y])

    def wanted_columns(z):
        return jnp.stack(
            [column(3 - z, 1 - core), column(z, 1 - core), column(3 - z, core), column(z, core)]
        )

    k_own, v_own, slots = project(image_features, key_weight, value_weight, selected)
    pieces = pick(wanted_columns(z ^ 1), after(output_weight, k_own), NEAR_PIECES)
    k_ring = spread(k_own, 1, 0, lambda part: after(part, pieces[0]))
    v_ring = spread(v_own, 0, 1)
    near_weight = []
    for piece in pieces:
        near_weight.append(to_near(after(piece, near_weight[-1] if near_weight else k_ring[3])))

    queries = queries_of(after(text_hidden, k_own), norm_gain, query_weight)

    k_out, v_out = pack(after(after(place, near_weight[0]), queries), k_ring, v_ring)
    keys = exchange(k_out, 0, 1)
    values = exchange(v_out, 1, 0, lambda part: after(part, near_weight[1]))
    own_weight = pick(
        wanted_columns(z), after(output_weight, k_out[0]), (output_weight.shape[0],)
    )
    weight = jnp.concatenate([*own_weight, *near_weight])

    starts = [sum(CHUNKS[:index]) for index in range(len(CHUNKS))]
    mine, near, sent, outs = [], [], [], []

    def attended(slots):
        index = len(mine)
        part = attend(starts[index], CHUNKS[index], slots, place, queries, keys, values)
        mine.append(part)
        near.append(to_near(part))
        return after(slots, part)

    while len(mine) < AHEAD:
        slots = attended(slots)
    weight = after(weight, mine[-1])
    last = len(CHUNKS) - 1
    for index in range(len(CHUNKS)):
        if index >= LAG:
            weight = after(weight, sent[index - LAG])
        if index >= 3:
            weight = after(weight, outs[index - 3])
        give_far, give_own, keep_far, keep_own = multiply(mine[index], near[index], weight)
        weight = after(weight, give_far)
        if len(mine) < len(CHUNKS):
            slots = attended(after(slots, give_far))
            weight = after(weight, mine[-1])
        got_far, got_own = to_core(give_far), to_core(give_own)
        if index >= 2 and index == last:
            got_far = after(got_far, outs[index - 2])
        send = (keep_far + got_far.astype(jnp.float32)).astype(jnp.bfloat16)
        far = to_far(send)
        sent.append(send)
        total = keep_own + got_own.astype(jnp.float32) + far.astype(jnp.float32)
        outs.append(total.astype(jnp.bfloat16))
    return jnp.concatenate(outs, axis=0)


def solution(mesh):
    in_specs = (
        P("seq", None),
        P(),
        P("seq", None),
        P(None, ("section", "head")),
        P(None, ("section", "head")),
        P(None, ("section", "head")),
        P(("section", "head"), None),
        P("seq", None),
    )
    out_specs = P("seq", ("section", "head"))
    return jax.shard_map(shards, mesh=mesh, in_specs=in_specs, out_specs=out_specs, check_vma=False)
```

```python
import functools

import jax
import jax.numpy as jnp
from jax import lax
from jax.experimental import pallas as pl
from jax.experimental.pallas import tpu as pltpu
from jax.sharding import PartitionSpec as P

HEADS = 32
KV_HEADS = 8
HEAD_DIM = 128
GROUP = HEADS // KV_HEADS
TILE = 128
BLOCK = 64
TOPK = 16
SIDE = 4
CAP = 8
PICKS = SIDE * SIDE * CAP
NOTE_ROWS = 16
EPSILON = 1e-05
NEAR_PIECES = (112, 144, 128, 128)
CHUNKS = (2, 2, 2, 2)
AHEAD = 3
LAG = 2
SCALE = HEAD_DIM**-0.5
LOG2_E = 1.4426950408889634

SECTION_HEAD = ("section", "head")
SMALL = pl.CostEstimate(flops=1, bytes_accessed=1, transcendentals=0)
VMEM_WHOLE = pl.BlockSpec(memory_space=pltpu.VMEM)
SMEM_WHOLE = pl.BlockSpec(memory_space=pltpu.SMEM)


def along_seq(value, dx, dy):
    pairs = [
        (x * SIDE + y, (x + dx) % SIDE * SIDE + (y + dy) % SIDE)
        for x in range(SIDE)
        for y in range(SIDE)
    ]
    return lax.ppermute(value, "seq", pairs)


def column(z, core):
    return (z % 2) * 4 + core * 2 + z // 2


def along_z(value, place):
    pairs = []
    for z in range(4):
        for core in range(2):
            pairs.append((column(z, core), column(*place(z, core))))
    return lax.ppermute(value, SECTION_HEAD, pairs)


def to_near(value):
    return along_z(value, lambda z, core: (z ^ 1, core))


def to_far(value):
    return along_z(value, lambda z, core: (3 - z, core))


def to_core(value):
    return along_z(value, lambda z, core: (z, 1 - core))


def project_body(selected_ref, x_ref, wk_ref, wv_ref, k_ref, v_ref, slots_ref, w_ref):
    step = pl.program_id(0)
    rows = x_ref.shape[0]
    steps = pl.num_programs(0)
    blocks_dev = (k_ref.shape[0] - NOTE_ROWS) // BLOCK
    blocks = SIDE * SIDE * blocks_dev

    @pl.when(step == 0)
    def _():
        w_ref[:, :HEAD_DIM] = wk_ref[...]
        w_ref[:, HEAD_DIM:] = wv_ref[...]
    @pl.when(step == steps - 1)
    def _():
        picked = selected_ref[...]
        tiles, per_tile = picked.shape
        source = lax.broadcasted_iota(jnp.int32, (per_tile, PICKS), 0)
        place = lax.broadcasted_iota(jnp.int32, (per_tile, PICKS), 1)
        repeat = (place % per_tile == source).astype(jnp.float32).astype(jnp.bfloat16)

        def repeated(part):
            part = part.astype(jnp.float32).astype(jnp.bfloat16)
            return jnp.dot(part, repeat, preferred_element_type=jnp.float32)

        wide = repeated(picked // blocks_dev) * blocks_dev + repeated(picked % blocks_dev)
        tile = lax.broadcasted_iota(jnp.int32, (tiles, PICKS), 0)
        at = lax.broadcasted_iota(jnp.int32, (tiles, PICKS), 1)
        ids = jnp.sum(jnp.where(at // per_tile == tile, wide, 0.0), axis=0, keepdims=True)

        block = lax.broadcasted_iota(jnp.int32, (blocks, PICKS), 0)
        hit = (block == ids.astype(jnp.int32)).astype(jnp.float32)
        wanted = jnp.broadcast_to(jnp.max(hit, axis=1, keepdims=True), (blocks, PICKS))
        one = lax.broadcasted_iota(jnp.int32, (blocks, blocks), 0)
        other = lax.broadcasted_iota(jnp.int32, (blocks, blocks), 1)
        before = (one // blocks_dev == other // blocks_dev) & (other < one)
        rank = jnp.dot(
            before.astype(jnp.float32).astype(jnp.bfloat16),
            wanted.astype(jnp.bfloat16),
            preferred_element_type=jnp.float32,
        )
        owner = block // blocks_dev
        slot = (owner * CAP).astype(jnp.float32) + rank
        slots = jnp.sum(hit * slot, axis=0, keepdims=True)
        slots_ref[...] = jnp.broadcast_to(slots, slots_ref.shape).astype(jnp.int32)
        place = lax.broadcasted_iota(jnp.int32, (blocks, PICKS), 1).astype(jnp.float32)
        local = (block % blocks_dev).astype(jnp.float32)
        asked = jnp.sum(
            jnp.where(slot == place, wanted * local, 0.0), axis=0, keepdims=True
        )
        note = jnp.broadcast_to(asked, (NOTE_ROWS, PICKS)).astype(jnp.bfloat16)
        k_ref[rows * steps :, :] = note
        v_ref[rows * steps :, :] = note

    both = jnp.dot(x_ref[...], w_ref[...], preferred_element_type=jnp.float32)
    at = pl.ds(pl.multiple_of(step * rows, rows), rows)
    k_ref[at, :] = both[:, :HEAD_DIM].astype(jnp.bfloat16)
    v_ref[at, :] = both[:, HEAD_DIM:].astype(jnp.bfloat16)


def in_hbm(value):
    return pltpu.with_memory_space_constraint(value, pltpu.HBM)


def project(image_features, key_weight, value_weight, selected):
    rows, enc = image_features.shape
    steps = 4
    out = jax.ShapeDtypeStruct((rows + NOTE_ROWS, HEAD_DIM), jnp.bfloat16)
    whole = lambda shape: pl.BlockSpec(shape, lambda i: (0,) * len(shape))
    return pl.pallas_call(
        project_body,
        grid=(steps,),
        in_specs=[
            whole(selected.shape),
            pl.BlockSpec((rows // steps, enc), lambda i: (i, 0)),
            whole((enc, HEAD_DIM)),
            whole((enc, HEAD_DIM)),
        ],
        out_specs=[
            whole((rows + NOTE_ROWS, HEAD_DIM)),
            whole((rows + NOTE_ROWS, HEAD_DIM)),
            whole((8, PICKS)),
        ],
        out_shape=[out, out, jax.ShapeDtypeStruct((8, PICKS), jnp.int32)],
        scratch_shapes=[pltpu.VMEM((enc, 2 * HEAD_DIM), jnp.bfloat16)],
        compiler_params=pltpu.CompilerParams(vmem_limit_bytes=40 << 20),
        cost_estimate=SMALL,
        name="project",
    )(selected, in_hbm(image_features), in_hbm(key_weight), in_hbm(value_weight))


def pack_one(ask, me, base, stride, ring, outs):
    for dest, out in enumerate(outs):
        for away, ref in enumerate(ring):
            first = base + ((me + away) & (SIDE - 1)) * stride
            for slot in range(CAP):
                block = pl.multiple_of(ask[dest, first + slot] * BLOCK, BLOCK)
                at = (away * CAP + slot) * BLOCK
                out[at : at + BLOCK, :] = ref[pl.ds(block, BLOCK), :]


def pack_body(place_ref, *refs):
    k_in, v_in, k_out, v_out = refs[:4], refs[4:8], refs[8:12], refs[12:16]
    note_ref, ask_ref, sem = refs[16:]

    def note(ring):
        last = lambda ref: ref[ref.shape[0] - NOTE_ROWS :, :].astype(jnp.float32)[:1]
        return jnp.concatenate([last(ref) for ref in ring], axis=0)

    notes = jnp.concatenate([note(v_in), note(k_in)], axis=0)
    note_ref[...] = notes.astype(jnp.int32)
    copy = pltpu.make_async_copy(note_ref, ask_ref, sem)
    copy.start()
    copy.wait()
    my_x, my_y = place_ref[0], place_ref[1]
    pack_one(ask_ref, my_x, my_y * CAP, SIDE * CAP, k_in, k_out)
    pack_one(ask_ref.at[SIDE:], my_y, my_x * (SIDE * CAP), CAP, v_in, v_out)


def pack(place, k_in, v_in):
    outs = [jax.ShapeDtypeStruct((SIDE * CAP * BLOCK, HEAD_DIM), jnp.bfloat16)] * SIDE
    out = pl.pallas_call(
        pack_body,
        in_specs=[SMEM_WHOLE] + [VMEM_WHOLE] * 8,
        out_specs=[VMEM_WHOLE] * 8,
        out_shape=outs + outs,
        scratch_shapes=[
            pltpu.VMEM((2 * SIDE, PICKS), jnp.int32),
            pltpu.SMEM((2 * SIDE, PICKS), jnp.int32),
            pltpu.SemaphoreType.DMA,
        ],
        compiler_params=pltpu.CompilerParams(vmem_limit_bytes=32 << 20),
        cost_estimate=SMALL,
        name="pack",
    )(place, *k_in, *v_in)
    return out[:4], out[4:]


def attend_body(first_tile, slots_ref, place_ref, q_ref, k_ref, v_ref, o_ref, kt, vt):
    my_x, my_y = place_ref[0], place_ref[1]
    for tile in range(o_ref.shape[0] // TILE):
        for pick in range(TOPK):
            slot = slots_ref[0, (first_tile + tile) * TOPK + pick]
            owner, rank = slot >> 3, slot & (CAP - 1)
            away_x = ((owner >> 2) - my_x) & (SIDE - 1)
            away_y = ((owner & 3) - my_y) & (SIDE - 1)
            k_at = (away_y * SIDE + away_x) * CAP + rank
            v_at = (away_x * SIDE + away_y) * CAP + rank
            to = slice(pick * BLOCK, (pick + 1) * BLOCK)
            kt[tile % 2, to, :] = k_ref[pl.ds(pl.multiple_of(k_at * BLOCK, BLOCK), BLOCK), :]
            vt[tile % 2, to, :] = v_ref[pl.ds(pl.multiple_of(v_at * BLOCK, BLOCK), BLOCK), :]
        rows = slice(tile * TILE, (tile + 1) * TILE)
        asking = slice((first_tile + tile) * TILE, (first_tile + tile + 1) * TILE)
        heads = [slice(h * HEAD_DIM, (h + 1) * HEAD_DIM) for h in range(GROUP)]
        stacked = jnp.concatenate([q_ref[asking, columns] for columns in heads], axis=0)
        scores = lax.dot_general(
            stacked, kt[tile % 2], (((1,), (1,)), ((), ())), preferred_element_type=jnp.float32
        )
        largest = jnp.max(scores, axis=-1, keepdims=True)
        exponent = jnp.exp2((scores - largest) * (SCALE * LOG2_E))
        total = jnp.sum(exponent, axis=-1, keepdims=True)
        weights = (exponent * (1.0 / total)).astype(jnp.bfloat16)
        mixed = jnp.dot(weights, vt[tile % 2], preferred_element_type=jnp.float32)
        mixed = mixed.astype(jnp.bfloat16)
        for h, columns in enumerate(heads):
            o_ref[rows, columns] = mixed[h * TILE : (h + 1) * TILE]


def attend(first_tile, tiles, slots, place, queries, keys, values):
    width = queries.shape[1]
    rows = tiles * TILE
    return pl.pallas_call(
        functools.partial(attend_body, first_tile),
        in_specs=[SMEM_WHOLE, SMEM_WHOLE] + [VMEM_WHOLE] * 3,
        out_specs=VMEM_WHOLE,
        out_shape=jax.ShapeDtypeStruct((rows, width), jnp.bfloat16),
        scratch_shapes=[pltpu.VMEM((2, TOPK * BLOCK, HEAD_DIM), jnp.bfloat16)] * 2,
        compiler_params=pltpu.CompilerParams(vmem_limit_bytes=32 << 20),
        cost_estimate=SMALL,
        name="attend",
    )(slots, place, queries, keys, values)


def pick_body(places_ref, w_ref, *out_refs):
    at = 0
    for ref in out_refs:
        ref[...] = w_ref[at : at + ref.shape[0], :]
        at += ref.shape[0]


def pick(places, weight, pieces):
    depth, width = weight.shape[0], weight.shape[1] // 8
    return pl.pallas_call(
        pick_body,
        grid_spec=pltpu.PrefetchScalarGridSpec(
            num_scalar_prefetch=1,
            grid=(4,),
            in_specs=[pl.BlockSpec((depth, width), lambda i, places: (0, places[i]))],
            out_specs=[pl.BlockSpec((rows, width), lambda i, places: (0, i)) for rows in pieces],
        ),
        out_shape=[jax.ShapeDtypeStruct((rows, 4 * width), weight.dtype) for rows in pieces],
        compiler_params=pltpu.CompilerParams(vmem_limit_bytes=8 << 20),
        cost_estimate=SMALL,
        name="pick",
    )(places, in_hbm(weight))


def multiply_body(mine_ref, near_ref, w_ref, *out_refs):
    left = jnp.concatenate([mine_ref[...], near_ref[...]], axis=1)
    width = w_ref.shape[1] // len(out_refs)
    for group, out_ref in enumerate(out_refs):
        columns = slice(group * width, (group + 1) * width)
        product = jnp.dot(left, w_ref[:, columns], preferred_element_type=jnp.float32)
        out_ref[...] = product.astype(out_ref.dtype)


def multiply(mine, near, weight):
    shape = (mine.shape[0], weight.shape[1] // 4)
    give = jax.ShapeDtypeStruct(shape, jnp.bfloat16)
    keep = jax.ShapeDtypeStruct(shape, jnp.float32)
    return pl.pallas_call(
        multiply_body,
        in_specs=[VMEM_WHOLE] * 3,
        out_specs=[VMEM_WHOLE] * 4,
        out_shape=[give, give, keep, keep],
        compiler_params=pltpu.CompilerParams(vmem_limit_bytes=24 << 20),
        cost_estimate=SMALL,
        name="multiply",
    )(mine, near, weight)


def ask_body(x_ref, gain_ref, w_ref, o_ref):
    as_float = x_ref[...].astype(jnp.float32)
    mean = jnp.mean(as_float * as_float, axis=-1, keepdims=True)
    normed = (as_float * lax.rsqrt(mean + EPSILON) * gain_ref[...]).astype(jnp.bfloat16)
    product = jnp.dot(normed, w_ref[...], preferred_element_type=jnp.float32)
    o_ref[...] = product.astype(jnp.bfloat16)


def queries_of(text_hidden, norm_gain, query_weight):
    (rows, depth), width = text_hidden.shape, query_weight.shape[1]
    steps = 4
    return pl.pallas_call(
        ask_body,
        grid=(steps,),
        in_specs=[
            pl.BlockSpec((rows // steps, depth), lambda i: (i, 0)),
            pl.BlockSpec((1, depth), lambda i: (0, 0)),
            pl.BlockSpec((depth, width), lambda i: (0, 0)),
        ],
        out_specs=pl.BlockSpec((rows // steps, width), lambda i: (i, 0)),
        out_shape=jax.ShapeDtypeStruct((rows, width), jnp.bfloat16),
        compiler_params=pltpu.CompilerParams(vmem_limit_bytes=32 << 20),
        cost_estimate=SMALL,
        name="ask",
    )(in_hbm(text_hidden), norm_gain.reshape(1, depth), in_hbm(query_weight))


def after(value, other):
    return lax.optimization_barrier((value, other))[0]


def spread(value, dx, dy, hold=lambda part: part):
    minus = along_seq(value, dx, dy)
    plus = along_seq(value, -dx, -dy)
    two = along_seq(hold(after(value, minus)), 2 * dx, 2 * dy)
    return value, plus, two, minus


def exchange(packed, dx, dy, hold=lambda part: part):
    here, up, across, down = packed
    minus = along_seq(up, dx, dy)
    plus = along_seq(down, -dx, -dy)
    two = along_seq(hold(after(across, minus)), 2 * dx, 2 * dy)
    return jnp.concatenate([here, plus, two, minus])


def shards(
    text_hidden,
    norm_gain,
    image_features,
    query_weight,
    key_weight,
    value_weight,
    output_weight,
    selected,
):
    seq = lax.axis_index("seq")
    my_x, my_y = seq // SIDE, seq % SIDE
    section, z_hi = lax.axis_index("section"), lax.axis_index("head")
    z, core = z_hi * 2 + section // 2, section % 2

    place = jnp.stack([my_x, my_y])

    def wanted_columns(z):
        return jnp.stack(
            [column(3 - z, 1 - core), column(z, 1 - core), column(3 - z, core), column(z, core)]
        )

    k_own, v_own, slots = project(image_features, key_weight, value_weight, selected)
    pieces = pick(wanted_columns(z ^ 1), after(output_weight, k_own), NEAR_PIECES)
    k_ring = spread(k_own, 1, 0, lambda part: after(part, pieces[0]))
    v_ring = spread(v_own, 0, 1)
    near_weight = []
    for piece in pieces:
        near_weight.append(to_near(after(piece, near_weight[-1] if near_weight else k_ring[3])))

    queries = queries_of(after(text_hidden, k_own), norm_gain, query_weight)

    k_out, v_out = pack(after(after(place, near_weight[0]), queries), k_ring, v_ring)
    keys = exchange(k_out, 0, 1)
    values = exchange(v_out, 1, 0, lambda part: after(part, near_weight[1]))
    own_weight = pick(
        wanted_columns(z), after(output_weight, k_out[0]), (output_weight.shape[0],)
    )
    weight = jnp.concatenate([*own_weight, *near_weight])

    starts = [sum(CHUNKS[:index]) for index in range(len(CHUNKS))]
    mine, near, sent, outs = [], [], [], []

    def attended(slots):
        index = len(mine)
        part = attend(starts[index], CHUNKS[index], slots, place, queries, keys, values)
        mine.append(part)
        near.append(to_near(part))
        return after(slots, part)

    while len(mine) < AHEAD:
        slots = attended(slots)
    weight = after(weight, mine[-1])
    last = len(CHUNKS) - 1
    for index in range(len(CHUNKS)):
        if index >= LAG:
            weight = after(weight, sent[index - LAG])
        if index >= 3:
            weight = after(weight, outs[index - 3])
        give_far, give_own, keep_far, keep_own = multiply(mine[index], near[index], weight)
        weight = after(weight, give_far)
        if len(mine) < len(CHUNKS):
            slots = attended(after(slots, give_far))
            weight = after(weight, mine[-1])
        got_far, got_own = to_core(give_far), to_core(give_own)
        if index >= 2 and index == last:
            got_far = after(got_far, outs[index - 2])
        send = (keep_far + got_far.astype(jnp.float32)).astype(jnp.bfloat16)
        far = to_far(send)
        sent.append(send)
        total = keep_own + got_own.astype(jnp.float32) + far.astype(jnp.float32)
        outs.append(total.astype(jnp.bfloat16))
    whole = jnp.zeros((sum(CHUNKS) * TILE, outs[0].shape[1]), outs[0].dtype)
    for start, part in zip(starts, outs):
        whole = lax.dynamic_update_slice_in_dim(whole, part, start * TILE, 0)
    return whole


def solution(mesh):
    in_specs = (
        P("seq", None),
        P(),
        P("seq", None),
        P(None, ("section", "head")),
        P(None, ("section", "head")),
        P(None, ("section", "head")),
        P(("section", "head"), None),
        P("seq", None),
    )
    out_specs = P("seq", ("section", "head"))
    return jax.shard_map(shards, mesh=mesh, in_specs=in_specs, out_specs=out_specs, check_vma=False)
```

```python
import functools

import jax
import jax.numpy as jnp
from jax import lax
from jax.experimental import pallas as pl
from jax.experimental.pallas import tpu as pltpu
from jax.sharding import PartitionSpec as P

HEADS = 32
KV_HEADS = 8
HEAD_DIM = 128
GROUP = HEADS // KV_HEADS
TILE = 128
BLOCK = 64
TOPK = 16
SIDE = 4
CAP = 8
PICKS = SIDE * SIDE * CAP
NOTE_ROWS = 16
EPSILON = 1e-05
NEAR_PIECES = (96, 144, 144, 128)
CHUNKS = (2, 2, 2, 2)
AHEAD = 3
LAG = 2
SCALE = HEAD_DIM**-0.5
LOG2_E = 1.4426950408889634

SECTION_HEAD = ("section", "head")
SMALL = pl.CostEstimate(flops=1, bytes_accessed=1, transcendentals=0)
VMEM_WHOLE = pl.BlockSpec(memory_space=pltpu.VMEM)
SMEM_WHOLE = pl.BlockSpec(memory_space=pltpu.SMEM)


def along_seq(value, dx, dy):
    pairs = [
        (x * SIDE + y, (x + dx) % SIDE * SIDE + (y + dy) % SIDE)
        for x in range(SIDE)
        for y in range(SIDE)
    ]
    return lax.ppermute(value, "seq", pairs)


def column(z, core):
    return (z % 2) * 4 + core * 2 + z // 2


def along_z(value, place):
    pairs = []
    for z in range(4):
        for core in range(2):
            pairs.append((column(z, core), column(*place(z, core))))
    return lax.ppermute(value, SECTION_HEAD, pairs)


def to_near(value):
    return along_z(value, lambda z, core: (z ^ 1, core))


def to_far(value):
    return along_z(value, lambda z, core: (3 - z, core))


def to_core(value):
    return along_z(value, lambda z, core: (z, 1 - core))


def project_body(selected_ref, x_ref, wk_ref, wv_ref, k_ref, v_ref, slots_ref, w_ref):
    step = pl.program_id(0)
    rows = x_ref.shape[0]
    steps = pl.num_programs(0)
    blocks_dev = (k_ref.shape[0] - NOTE_ROWS) // BLOCK
    blocks = SIDE * SIDE * blocks_dev

    @pl.when(step == 0)
    def _():
        w_ref[:, :HEAD_DIM] = wk_ref[...]
        w_ref[:, HEAD_DIM:] = wv_ref[...]
    @pl.when(step == steps - 1)
    def _():
        picked = selected_ref[...]
        tiles, per_tile = picked.shape
        source = lax.broadcasted_iota(jnp.int32, (per_tile, PICKS), 0)
        place = lax.broadcasted_iota(jnp.int32, (per_tile, PICKS), 1)
        repeat = (place % per_tile == source).astype(jnp.float32).astype(jnp.bfloat16)

        def repeated(part):
            part = part.astype(jnp.float32).astype(jnp.bfloat16)
            return jnp.dot(part, repeat, preferred_element_type=jnp.float32)

        wide = repeated(picked // blocks_dev) * blocks_dev + repeated(picked % blocks_dev)
        tile = lax.broadcasted_iota(jnp.int32, (tiles, PICKS), 0)
        at = lax.broadcasted_iota(jnp.int32, (tiles, PICKS), 1)
        ids = jnp.sum(jnp.where(at // per_tile == tile, wide, 0.0), axis=0, keepdims=True)

        block = lax.broadcasted_iota(jnp.int32, (blocks, PICKS), 0)
        hit = (block == ids.astype(jnp.int32)).astype(jnp.float32)
        wanted = jnp.broadcast_to(jnp.max(hit, axis=1, keepdims=True), (blocks, PICKS))
        one = lax.broadcasted_iota(jnp.int32, (blocks, blocks), 0)
        other = lax.broadcasted_iota(jnp.int32, (blocks, blocks), 1)
        before = (one // blocks_dev == other // blocks_dev) & (other < one)
        rank = jnp.dot(
            before.astype(jnp.float32).astype(jnp.bfloat16),
            wanted.astype(jnp.bfloat16),
            preferred_element_type=jnp.float32,
        )
        owner = block // blocks_dev
        slot = (owner * CAP).astype(jnp.float32) + rank
        slots = jnp.sum(hit * slot, axis=0, keepdims=True)
        slots_ref[...] = jnp.broadcast_to(slots, slots_ref.shape).astype(jnp.int32)
        place = lax.broadcasted_iota(jnp.int32, (blocks, PICKS), 1).astype(jnp.float32)
        local = (block % blocks_dev).astype(jnp.float32)
        asked = jnp.sum(
            jnp.where(slot == place, wanted * local, 0.0), axis=0, keepdims=True
        )
        note = jnp.broadcast_to(asked, (NOTE_ROWS, PICKS)).astype(jnp.bfloat16)
        k_ref[rows * steps :, :] = note
        v_ref[rows * steps :, :] = note

    both = jnp.dot(x_ref[...], w_ref[...], preferred_element_type=jnp.float32)
    at = pl.ds(pl.multiple_of(step * rows, rows), rows)
    k_ref[at, :] = both[:, :HEAD_DIM].astype(jnp.bfloat16)
    v_ref[at, :] = both[:, HEAD_DIM:].astype(jnp.bfloat16)


def in_hbm(value):
    return pltpu.with_memory_space_constraint(value, pltpu.HBM)


def project(image_features, key_weight, value_weight, selected):
    rows, enc = image_features.shape
    steps = 4
    out = jax.ShapeDtypeStruct((rows + NOTE_ROWS, HEAD_DIM), jnp.bfloat16)
    whole = lambda shape: pl.BlockSpec(shape, lambda i: (0,) * len(shape))
    return pl.pallas_call(
        project_body,
        grid=(steps,),
        in_specs=[
            whole(selected.shape),
            pl.BlockSpec((rows // steps, enc), lambda i: (i, 0)),
            whole((enc, HEAD_DIM)),
            whole((enc, HEAD_DIM)),
        ],
        out_specs=[
            whole((rows + NOTE_ROWS, HEAD_DIM)),
            whole((rows + NOTE_ROWS, HEAD_DIM)),
            whole((8, PICKS)),
        ],
        out_shape=[out, out, jax.ShapeDtypeStruct((8, PICKS), jnp.int32)],
        scratch_shapes=[pltpu.VMEM((enc, 2 * HEAD_DIM), jnp.bfloat16)],
        compiler_params=pltpu.CompilerParams(vmem_limit_bytes=40 << 20),
        cost_estimate=SMALL,
        name="project",
    )(selected, in_hbm(image_features), in_hbm(key_weight), in_hbm(value_weight))


def pack_one(ask, me, base, stride, ring, outs):
    for dest, out in enumerate(outs):
        for away, ref in enumerate(ring):
            first = base + ((me + away) & (SIDE - 1)) * stride
            for slot in range(CAP):
                block = pl.multiple_of(ask[dest, first + slot] * BLOCK, BLOCK)
                at = (away * CAP + slot) * BLOCK
                out[at : at + BLOCK, :] = ref[pl.ds(block, BLOCK), :]


def pack_body(place_ref, *refs):
    k_in, v_in, k_out, v_out = refs[:4], refs[4:8], refs[8:12], refs[12:16]
    note_ref, ask_ref, sem = refs[16:]

    def note(ring):
        last = lambda ref: ref[ref.shape[0] - NOTE_ROWS :, :].astype(jnp.float32)[:1]
        return jnp.concatenate([last(ref) for ref in ring], axis=0)

    notes = jnp.concatenate([note(v_in), note(k_in)], axis=0)
    note_ref[...] = notes.astype(jnp.int32)
    copy = pltpu.make_async_copy(note_ref, ask_ref, sem)
    copy.start()
    copy.wait()
    my_x, my_y = place_ref[0], place_ref[1]
    pack_one(ask_ref, my_x, my_y * CAP, SIDE * CAP, k_in, k_out)
    pack_one(ask_ref.at[SIDE:], my_y, my_x * (SIDE * CAP), CAP, v_in, v_out)


def pack(place, k_in, v_in):
    outs = [jax.ShapeDtypeStruct((SIDE * CAP * BLOCK, HEAD_DIM), jnp.bfloat16)] * SIDE
    out = pl.pallas_call(
        pack_body,
        in_specs=[SMEM_WHOLE] + [VMEM_WHOLE] * 8,
        out_specs=[VMEM_WHOLE] * 8,
        out_shape=outs + outs,
        scratch_shapes=[
            pltpu.VMEM((2 * SIDE, PICKS), jnp.int32),
            pltpu.SMEM((2 * SIDE, PICKS), jnp.int32),
            pltpu.SemaphoreType.DMA,
        ],
        compiler_params=pltpu.CompilerParams(vmem_limit_bytes=32 << 20),
        cost_estimate=SMALL,
        name="pack",
    )(place, *k_in, *v_in)
    return out[:4], out[4:]


def attend_body(first_tile, slots_ref, place_ref, q_ref, k_ref, v_ref, o_ref, kt, vt):
    my_x, my_y = place_ref[0], place_ref[1]
    for tile in range(o_ref.shape[0] // TILE):
        for pick in range(TOPK):
            slot = slots_ref[0, (first_tile + tile) * TOPK + pick]
            owner, rank = slot >> 3, slot & (CAP - 1)
            away_x = ((owner >> 2) - my_x) & (SIDE - 1)
            away_y = ((owner & 3) - my_y) & (SIDE - 1)
            k_at = (away_y * SIDE + away_x) * CAP + rank
            v_at = (away_x * SIDE + away_y) * CAP + rank
            to = slice(pick * BLOCK, (pick + 1) * BLOCK)
            kt[tile % 2, to, :] = k_ref[pl.ds(pl.multiple_of(k_at * BLOCK, BLOCK), BLOCK), :]
            vt[tile % 2, to, :] = v_ref[pl.ds(pl.multiple_of(v_at * BLOCK, BLOCK), BLOCK), :]
        rows = slice(tile * TILE, (tile + 1) * TILE)
        asking = slice((first_tile + tile) * TILE, (first_tile + tile + 1) * TILE)
        heads = [slice(h * HEAD_DIM, (h + 1) * HEAD_DIM) for h in range(GROUP)]
        stacked = jnp.concatenate([q_ref[asking, columns] for columns in heads], axis=0)
        scores = lax.dot_general(
            stacked, kt[tile % 2], (((1,), (1,)), ((), ())), preferred_element_type=jnp.float32
        )
        largest = jnp.max(scores, axis=-1, keepdims=True)
        exponent = jnp.exp2((scores - largest) * (SCALE * LOG2_E))
        total = jnp.sum(exponent, axis=-1, keepdims=True)
        weights = (exponent * (1.0 / total)).astype(jnp.bfloat16)
        mixed = jnp.dot(weights, vt[tile % 2], preferred_element_type=jnp.float32)
        mixed = mixed.astype(jnp.bfloat16)
        for h, columns in enumerate(heads):
            o_ref[rows, columns] = mixed[h * TILE : (h + 1) * TILE]


def attend(first_tile, tiles, slots, place, queries, keys, values):
    width = queries.shape[1]
    rows = tiles * TILE
    return pl.pallas_call(
        functools.partial(attend_body, first_tile),
        in_specs=[SMEM_WHOLE, SMEM_WHOLE] + [VMEM_WHOLE] * 3,
        out_specs=VMEM_WHOLE,
        out_shape=jax.ShapeDtypeStruct((rows, width), jnp.bfloat16),
        scratch_shapes=[pltpu.VMEM((2, TOPK * BLOCK, HEAD_DIM), jnp.bfloat16)] * 2,
        compiler_params=pltpu.CompilerParams(vmem_limit_bytes=32 << 20),
        cost_estimate=SMALL,
        name="attend",
    )(slots, place, queries, keys, values)


def pick_body(places_ref, w_ref, *out_refs):
    at = 0
    for ref in out_refs:
        ref[...] = w_ref[at : at + ref.shape[0], :]
        at += ref.shape[0]


def pick(places, weight, pieces):
    depth, width = weight.shape[0], weight.shape[1] // 8
    return pl.pallas_call(
        pick_body,
        grid_spec=pltpu.PrefetchScalarGridSpec(
            num_scalar_prefetch=1,
            grid=(4,),
            in_specs=[pl.BlockSpec((depth, width), lambda i, places: (0, places[i]))],
            out_specs=[pl.BlockSpec((rows, width), lambda i, places: (0, i)) for rows in pieces],
        ),
        out_shape=[jax.ShapeDtypeStruct((rows, 4 * width), weight.dtype) for rows in pieces],
        compiler_params=pltpu.CompilerParams(vmem_limit_bytes=8 << 20),
        cost_estimate=SMALL,
        name="pick",
    )(places, in_hbm(weight))


def multiply_body(mine_ref, near_ref, w_ref, *out_refs):
    left = jnp.concatenate([mine_ref[...], near_ref[...]], axis=1)
    width = w_ref.shape[1] // len(out_refs)
    for group, out_ref in enumerate(out_refs):
        columns = slice(group * width, (group + 1) * width)
        product = jnp.dot(left, w_ref[:, columns], preferred_element_type=jnp.float32)
        out_ref[...] = product.astype(out_ref.dtype)


def multiply(mine, near, weight):
    shape = (mine.shape[0], weight.shape[1] // 4)
    give = jax.ShapeDtypeStruct(shape, jnp.bfloat16)
    keep = jax.ShapeDtypeStruct(shape, jnp.float32)
    return pl.pallas_call(
        multiply_body,
        in_specs=[VMEM_WHOLE] * 3,
        out_specs=[VMEM_WHOLE] * 4,
        out_shape=[give, give, keep, keep],
        compiler_params=pltpu.CompilerParams(vmem_limit_bytes=24 << 20),
        cost_estimate=SMALL,
        name="multiply",
    )(mine, near, weight)


def ask_body(x_ref, gain_ref, w_ref, o_ref):
    as_float = x_ref[...].astype(jnp.float32)
    mean = jnp.mean(as_float * as_float, axis=-1, keepdims=True)
    normed = (as_float * lax.rsqrt(mean + EPSILON) * gain_ref[...]).astype(jnp.bfloat16)
    product = jnp.dot(normed, w_ref[...], preferred_element_type=jnp.float32)
    o_ref[...] = product.astype(jnp.bfloat16)


def queries_of(text_hidden, norm_gain, query_weight):
    (rows, depth), width = text_hidden.shape, query_weight.shape[1]
    steps = 8
    return pl.pallas_call(
        ask_body,
        grid=(steps,),
        in_specs=[
            pl.BlockSpec((rows // steps, depth), lambda i: (i, 0)),
            pl.BlockSpec((1, depth), lambda i: (0, 0)),
            pl.BlockSpec((depth, width), lambda i: (0, 0)),
        ],
        out_specs=pl.BlockSpec((rows // steps, width), lambda i: (i, 0)),
        out_shape=jax.ShapeDtypeStruct((rows, width), jnp.bfloat16),
        compiler_params=pltpu.CompilerParams(vmem_limit_bytes=32 << 20),
        cost_estimate=SMALL,
        name="ask",
    )(in_hbm(text_hidden), norm_gain.reshape(1, depth), in_hbm(query_weight))


def after(value, other):
    return lax.optimization_barrier((value, other))[0]


def spread(value, dx, dy, hold=lambda part: part):
    minus = along_seq(value, dx, dy)
    plus = along_seq(value, -dx, -dy)
    two = along_seq(hold(after(value, minus)), 2 * dx, 2 * dy)
    return value, plus, two, minus


def exchange(packed, dx, dy, hold=lambda part: part):
    here, up, across, down = packed
    minus = along_seq(up, dx, dy)
    plus = along_seq(down, -dx, -dy)
    two = along_seq(hold(after(across, minus)), 2 * dx, 2 * dy)
    return jnp.concatenate([here, plus, two, minus])


def shards(
    text_hidden,
    norm_gain,
    image_features,
    query_weight,
    key_weight,
    value_weight,
    output_weight,
    selected,
):
    seq = lax.axis_index("seq")
    my_x, my_y = seq // SIDE, seq % SIDE
    section, z_hi = lax.axis_index("section"), lax.axis_index("head")
    z, core = z_hi * 2 + section // 2, section % 2

    place = jnp.stack([my_x, my_y])

    def wanted_columns(z):
        return jnp.stack(
            [column(3 - z, 1 - core), column(z, 1 - core), column(3 - z, core), column(z, core)]
        )

    k_own, v_own, slots = project(image_features, key_weight, value_weight, selected)
    pieces = pick(wanted_columns(z ^ 1), after(output_weight, k_own), NEAR_PIECES)
    k_ring = spread(k_own, 1, 0, lambda part: after(part, pieces[0]))
    v_ring = spread(v_own, 0, 1)
    near_weight = []
    for piece in pieces:
        near_weight.append(to_near(after(piece, near_weight[-1] if near_weight else k_ring[3])))

    queries = queries_of(after(text_hidden, k_own), norm_gain, query_weight)

    k_out, v_out = pack(after(after(place, near_weight[0]), queries), k_ring, v_ring)
    keys = exchange(k_out, 0, 1)
    values = exchange(v_out, 1, 0, lambda part: after(part, near_weight[1]))
    own_weight = pick(
        wanted_columns(z), after(output_weight, k_out[0]), (output_weight.shape[0],)
    )
    weight = jnp.concatenate([*own_weight, *near_weight])

    starts = [sum(CHUNKS[:index]) for index in range(len(CHUNKS))]
    mine, near, sent, outs = [], [], [], []

    def attended(slots):
        index = len(mine)
        part = attend(starts[index], CHUNKS[index], slots, place, queries, keys, values)
        mine.append(part)
        near.append(to_near(part))
        return after(slots, part)

    while len(mine) < AHEAD:
        slots = attended(slots)
    weight = after(weight, mine[-1])
    last = len(CHUNKS) - 1
    for index in range(len(CHUNKS)):
        if index >= LAG:
            weight = after(weight, sent[index - LAG])
        if index >= 3:
            weight = after(weight, outs[index - 3])
        give_far, give_own, keep_far, keep_own = multiply(mine[index], near[index], weight)
        weight = after(weight, give_far)
        if len(mine) < len(CHUNKS):
            slots = attended(after(slots, give_far))
            weight = after(weight, mine[-1])
        got_far, got_own = to_core(give_far), to_core(give_own)
        if index >= 2 and index == last:
            got_far = after(got_far, outs[index - 2])
        send = (keep_far + got_far.astype(jnp.float32)).astype(jnp.bfloat16)
        far = to_far(send)
        sent.append(send)
        total = keep_own + got_own.astype(jnp.float32) + far.astype(jnp.float32)
        outs.append(total.astype(jnp.bfloat16))
    return jnp.concatenate(outs, axis=0)


def solution(mesh):
    in_specs = (
        P("seq", None),
        P(),
        P("seq", None),
        P(None, ("section", "head")),
        P(None, ("section", "head")),
        P(None, ("section", "head")),
        P(("section", "head"), None),
        P("seq", None),
    )
    out_specs = P("seq", ("section", "head"))
    return jax.shard_map(shards, mesh=mesh, in_specs=in_specs, out_specs=out_specs, check_vma=False)
```
